32 devices in a mesh: pipe: 4 (over x, core), expert: 8 (over z, y).
Axes of the slice: x: 2, y: 2, z: 4, core: 2. Of those that a mesh axis runs over, the one named last changes fastest.
Arguments:
- x_prev_a: bfloat16 [4, 256, 2048], P('pipe', 'expert'), may hold values from -6 to 6
- route_a: int32 [4, 256, 8], P('pipe', 'expert'), may hold values from 0 to 7, as said below
- prob_a: int32 [4, 256, 8], P('pipe', 'expert'), may hold values from 1 to 255
- w_gate: bfloat16 [8, 2048, 768], P('expert'), may hold values from -0.125 to 0.125
- w_up: bfloat16 [8, 2048, 768], P('expert'), may hold values from -0.125 to 0.125
- route_b: int32 [4, 256, 8], P('pipe', 'expert'), may hold values from 0 to 7, as said below
- prob_b: bfloat16 [4, 8, 8, 32], P('pipe', 'expert'), may hold values from 0.049804688 to 1
- saved_gate_b: bfloat16 [4, 8, 8, 32, 768], P('pipe', 'expert'), may hold values from -6 to 6
- saved_up_b: bfloat16 [4, 8, 8, 32, 768], P('pipe', 'expert'), may hold values from -6 to 6
- grad_hidden_b: bfloat16 [4, 8, 8, 32, 768], P('pipe', 'expert'), may hold values from -6 to 6
Outputs:
- hidden_a: bfloat16 [4, 8, 8, 32, 768], P('pipe', 'expert')
- grad_x_b: bfloat16 [4, 256, 2048], P('pipe', 'expert')
- grad_prob_b: bfloat16 [4, 256, 8], P('pipe', 'expert')
The draws below stay inside these ranges and needn't reach their ends.
Inputs may be any that keep to these rules, and one draw needn't show every extreme that they name: `route_a`: each token names 8 different experts. `route_b`: each token names 8 different experts.
All inputs are finite; a program needn't handle non-finite values.
Results may differ from the reference program's by a relative error of at most 0.0057.
Values may be sent and summed in bfloat16 or wider, within the bound.
A program may use at most 64 MiB of HBM per device.

```python
import jax
import jax.numpy as jnp
from jax import lax

D = 2048
H = 768
TOP = 8
TOK_DEV = 32
EXPERTS = 8
PIPE = 4
TOKENS = 256
CAP = 32


def routing_draw(key):
    level_key, hot_key, noise_key = jax.random.split(key, 3)
    levels = jax.random.randint(level_key, (PIPE, 1, EXPERTS), 0, 4) * 1024
    hottest = jax.random.randint(hot_key, (PIPE, 1, 1), 0, EXPERTS)
    noise_draw = jax.random.randint(noise_key, (PIPE, TOKENS, EXPERTS), 0, 2048)
    column = jnp.arange(EXPERTS, dtype=jnp.int32)[None, None, :]
    scores = (noise_draw + levels) * EXPERTS + column + jnp.where(column == hottest, 1 << 24, 0)
    ranked_scores, chosen = lax.top_k(scores, TOP)
    return chosen.astype(jnp.int32)


def draw_route_a(key, part):
    return routing_draw(jax.random.fold_in(key, 11))


def draw_route_b(key, part):
    return routing_draw(jax.random.fold_in(key, 23))


def place_ends(entries, rng, least, high):
    spot = [jax.random.randint(jax.random.fold_in(rng, axis), (), 0, length) for axis, length in enumerate(entries.shape)]
    longest = entries.shape.index(max(entries.shape))
    next_to = spot[:longest] + [(spot[longest] + 1) % entries.shape[longest]] + spot[longest + 1:]
    return entries.at[tuple(spot)].set(least).at[tuple(next_to)].set(high)


def shard_levels(key, extent, cuts, smallest, top_value):
    loudness = 1.0
    for position, shards_of in cuts:
        steps = jax.random.uniform(jax.random.fold_in(jax.random.fold_in(key, 6), position), (shards_of,), jnp.float32, smallest / len(cuts), top_value / len(cuts))
        loudness = loudness * jnp.repeat(jnp.exp(steps), extent[position] // shards_of).reshape((-1,) + (1,) * (len(extent) - 1 - position))
    return loudness


def scatter_about(stream_key, extent, scale, most, shards=(), held_as=jnp.bfloat16):
    entries = jax.random.normal(stream_key, extent, jnp.float32) * scale
    if len(shards) > 0:
        entries = shard_levels(stream_key, extent, shards, -0.22, 0.18) * entries
    return jnp.clip(entries, min=-most, max=most).astype(held_as)


def setup_inputs(seed: int = 0) -> dict:
    key_list = jax.random.split(jax.random.key(seed), 11)
    x_prev_a = scatter_about(key_list[0], (PIPE, TOKENS, D), 1.0, 6.0, ((0, 4), (1, 8)))
    route_a = draw_route_a(jax.random.fold_in(key_list[10], 71), 0)
    prob_a = place_ends(jax.random.randint(key_list[2], (PIPE, TOKENS, TOP), 1, 256), jax.random.fold_in(key_list[2], 1), 1, 255).astype(jnp.int32)
    w_gate = scatter_about(key_list[3], (EXPERTS, D, H), D ** -0.5, 0.125, ((0, 8),))
    w_up = scatter_about(key_list[4], (EXPERTS, D, H), D ** -0.5, 0.125, ((0, 8),))
    route_b = draw_route_b(jax.random.fold_in(key_list[10], 71), 0)
    prob_b = jnp.clip(0.049804688 + 0.9501953 * jax.random.uniform(key_list[6], (PIPE, EXPERTS, EXPERTS, CAP), jnp.float32) ** shard_levels(key_list[6], (PIPE, EXPERTS, EXPERTS, CAP), ((0, 4), (1, 8)), -0.2, 0.2), 0.049804688, 1.0).astype(jnp.bfloat16)
    saved_gate_b = scatter_about(key_list[7], (PIPE, EXPERTS, EXPERTS, CAP, H), 1.0, 6.0, ((0, 4), (1, 8)))
    saved_up_b = scatter_about(key_list[8], (PIPE, EXPERTS, EXPERTS, CAP, H), 1.0, 6.0, ((0, 4), (1, 8)))
    grad_hidden_b = scatter_about(key_list[9], (PIPE, EXPERTS, EXPERTS, CAP, H), 1.0, 6.0, ((0, 4), (1, 8)))
    return {"x_prev_a": x_prev_a, "route_a": route_a, "prob_a": prob_a, "w_gate": w_gate, "w_up": w_up, "route_b": route_b, "prob_b": prob_b, "saved_gate_b": saved_gate_b, "saved_up_b": saved_up_b, "grad_hidden_b": grad_hidden_b}


def slot_targets(block_ids):
    flat_ids = block_ids.reshape(-1)
    onehot = (flat_ids[:, None] == jnp.arange(EXPERTS, dtype=jnp.int32)[None, :]).astype(jnp.int32)
    before = jnp.cumsum(onehot, axis=0) - onehot
    slot_rank = jnp.sum(before * onehot, axis=1)
    target = jnp.where(slot_rank < CAP, flat_ids * CAP + slot_rank, -1)
    return target.reshape(block_ids.shape).astype(jnp.int32)


def flat_index(route_section):
    blocks = route_section.reshape(EXPERTS, TOK_DEV, TOP)
    target = jax.vmap(slot_targets)(blocks)
    source = jnp.arange(EXPERTS, dtype=jnp.int32)[:, None, None]
    spot = (target // CAP) * (EXPERTS * CAP) + source * CAP + target % CAP
    return jnp.where(target >= 0, spot, EXPERTS * EXPERTS * CAP).astype(jnp.int32)


def section_forward(operands, w_gate, w_up):
    x_section, route_section, quant_section = operands
    index = flat_index(route_section).reshape(-1)
    rows = jnp.broadcast_to(x_section.reshape(TOKENS, 1, D), (TOKENS, TOP, D)).reshape(-1, D)
    buffer = jnp.zeros((EXPERTS * EXPERTS * CAP + 1, D), jnp.bfloat16).at[index].set(rows)
    buffer = buffer[:-1].reshape(EXPERTS, EXPERTS * CAP, D)
    scales = jnp.zeros((EXPERTS * EXPERTS * CAP + 1,), jnp.float32).at[index].set(
        quant_section.reshape(-1).astype(jnp.float32) / 256.0)
    scales = scales[:-1].reshape(EXPERTS, EXPERTS * CAP)

    def one_expert(pieces):
        expert_rows, expert_scale, gate_weight, up_weight = pieces
        gate = jnp.dot(expert_rows, gate_weight, preferred_element_type=jnp.float32)
        up_proj = jnp.dot(expert_rows, up_weight, preferred_element_type=jnp.float32)
        return (expert_scale[:, None] * jax.nn.silu(gate) * up_proj).astype(jnp.bfloat16)

    hidden = lax.map(one_expert, (buffer, scales, w_gate, w_up))
    return hidden.reshape(EXPERTS, EXPERTS, CAP, H)


def section_backward(operands, w_gate, w_up):
    route_section, prob_section, gate_saved, up_saved, grad_hidden = operands

    def one_expert(pieces):
        gate_rows, up_rows, grad_rows, prob_rows, gate_weight, up_weight = pieces
        g_val = gate_rows.reshape(-1, H).astype(jnp.float32)
        u_val = up_rows.reshape(-1, H).astype(jnp.float32)
        dh_val = grad_rows.reshape(-1, H).astype(jnp.float32)
        p_val = prob_rows.reshape(-1, 1).astype(jnp.float32)
        sigma = jax.nn.sigmoid(g_val)
        active = g_val * sigma
        scaled = dh_val * p_val
        d_up = (scaled * active).astype(jnp.bfloat16)
        d_gate = (scaled * u_val * sigma * (1.0 + g_val * (1.0 - sigma))).astype(jnp.bfloat16)
        slot_dx = (jnp.einsum("rh,dh->rd", d_gate, gate_weight, preferred_element_type=jnp.float32)
                   + jnp.einsum("rh,dh->rd", d_up, up_weight, preferred_element_type=jnp.float32)).astype(jnp.bfloat16)
        slot_dp = jnp.sum(dh_val * active * u_val, axis=1).astype(jnp.bfloat16)
        return slot_dx, slot_dp

    slot_dx, slot_dp = lax.map(one_expert, (gate_saved, up_saved, grad_hidden, prob_section, w_gate, w_up))
    flat_dx = jnp.concatenate([slot_dx.reshape(-1, D), jnp.zeros((1, D), jnp.bfloat16)], axis=0)
    flat_dp = jnp.concatenate([slot_dp.reshape(-1), jnp.zeros((1,), jnp.bfloat16)], axis=0)
    index = flat_index(route_section).reshape(TOKENS, TOP)
    picked = jnp.take(flat_dx, index, axis=0).astype(jnp.float32)
    grad_tokens = jnp.sum(picked, axis=1).astype(jnp.bfloat16)
    grad_prob = jnp.take(flat_dp, index, axis=0)
    return grad_tokens, grad_prob


def reference(x_prev_a, route_a, prob_a, w_gate, w_up, route_b, prob_b, saved_gate_b, saved_up_b, grad_hidden_b):
    x_input = jnp.roll(x_prev_a, 1, axis=0)
    hidden_a = lax.map(lambda operands: section_forward(operands, w_gate, w_up), (x_input, route_a, prob_a))
    grads, grad_prob_b = lax.map(lambda operands: section_backward(operands, w_gate, w_up),
                                 (route_b, prob_b, saved_gate_b, saved_up_b, grad_hidden_b))
    grad_x_b = jnp.roll(grads, -1, axis=0)
    return hidden_a, grad_x_b, grad_prob_b
```

```python
import functools

import jax
import jax.numpy as jnp
from jax import lax
from jax.experimental import pallas as pl
from jax.experimental.pallas import tpu as pltpu
from jax.sharding import PartitionSpec as P


def passed_along(block, axis, distance):
    devices = range(lax.axis_size(axis))
    route = [((i - distance) % len(devices), i) for i in devices]
    return lax.ppermute(block, axis, route)


def slot_choice(route, capacity, experts):
    expert_ids = route[0]
    tok_rows, top_k = expert_ids.shape
    flat_ids = expert_ids.reshape(-1)
    onehot = (flat_ids[:, None] == jnp.arange(experts, dtype=jnp.int32)[None, :]).astype(jnp.int32)
    rows = flat_ids.shape[0]
    earlier = jnp.arange(rows)[:, None] > jnp.arange(rows)[None, :]
    before = jnp.dot(
        earlier.astype(jnp.bfloat16),
        onehot.astype(jnp.bfloat16),
        preferred_element_type=jnp.float32,
    ).astype(jnp.int32)
    slot_rank = jnp.sum(before * onehot, axis=1)
    target = jnp.where(slot_rank < capacity, flat_ids * capacity + slot_rank, -1).reshape(
        tok_rows, top_k
    )
    slot_ids = jnp.arange(experts * capacity, dtype=jnp.int32)
    return (target[:, :, None] == slot_ids[None, None, :]).astype(jnp.float32)


def dispatch_rows(tokens, route, quant, capacity, experts):
    chosen = slot_choice(route, capacity, experts)
    picker = jnp.sum(chosen, axis=1).astype(jnp.bfloat16)
    send_x = jnp.einsum("ts,td->sd", picker, tokens[0], preferred_element_type=jnp.float32).astype(
        jnp.bfloat16
    )
    send_p = (jnp.einsum("tks,tk->s", chosen, quant[0].astype(jnp.float32)) / 256.0).astype(
        jnp.bfloat16
    )
    return (send_x.reshape(experts, capacity, -1), send_p.reshape(experts, capacity))


def per_device(
    x_prev_a,
    route_a,
    prob_a,
    w_gate,
    w_up,
    route_b,
    prob_b,
    saved_gate_b,
    saved_up_b,
    grad_hidden_b,
):
    experts = lax.axis_size("expert")
    capacity = saved_gate_b.shape[3]
    width = x_prev_a.shape[2]
    units = saved_gate_b.shape[4]
    gate_weight = w_gate[0]
    up_weight = w_up[0]
    x_here = passed_along(x_prev_a, "pipe", 1)
    send_x, send_p = dispatch_rows(x_here, route_a, prob_a, capacity, experts)
    recv_x, recv_p = (
        lax.all_to_all(send_x, "expert", split_axis=0, concat_axis=0, tiled=True),
        lax.all_to_all(send_p, "expert", split_axis=0, concat_axis=0, tiled=True),
    )
    rows = recv_x.reshape(-1, width)
    gate = jnp.dot(rows, gate_weight, preferred_element_type=jnp.float32)
    up_proj = jnp.dot(rows, up_weight, preferred_element_type=jnp.float32)
    scale = recv_p.reshape(-1, 1).astype(jnp.float32)
    hidden = (scale * jax.nn.silu(gate) * up_proj).astype(jnp.bfloat16)
    hidden_a = hidden.reshape(1, 1, experts, capacity, units)
    g_val = saved_gate_b[0, 0].reshape(-1, units).astype(jnp.float32)
    u_val = saved_up_b[0, 0].reshape(-1, units).astype(jnp.float32)
    dh_val = grad_hidden_b[0, 0].reshape(-1, units).astype(jnp.float32)
    p_val = prob_b[0, 0].reshape(-1, 1).astype(jnp.float32)
    sigma = jax.nn.sigmoid(g_val)
    active = g_val * sigma
    scaled = dh_val * p_val
    d_up = (scaled * active).astype(jnp.bfloat16)
    d_gate = (scaled * u_val * sigma * (1.0 + g_val * (1.0 - sigma))).astype(jnp.bfloat16)
    slot_dx = (
        jnp.einsum("rh,dh->rd", d_gate, gate_weight, preferred_element_type=jnp.float32)
        + jnp.einsum("rh,dh->rd", d_up, up_weight, preferred_element_type=jnp.float32)
    ).astype(jnp.bfloat16)
    slot_dp = jnp.sum(dh_val * active * u_val, axis=1).astype(jnp.bfloat16)
    back_x, back_p = (
        lax.all_to_all(
            slot_dx.reshape(experts, capacity, width),
            "expert",
            split_axis=0,
            concat_axis=0,
            tiled=True,
        ),
        lax.all_to_all(
            slot_dp.reshape(experts, capacity), "expert", split_axis=0, concat_axis=0, tiled=True
        ),
    )
    chosen_b = slot_choice(route_b, capacity, experts)
    picker_b = jnp.sum(chosen_b, axis=1).astype(jnp.bfloat16)
    grad_tokens = jnp.dot(
        picker_b, back_x.reshape(-1, width), preferred_element_type=jnp.float32
    ).astype(jnp.bfloat16)
    grad_prob = jnp.einsum("tks,s->tk", chosen_b, back_p.reshape(-1).astype(jnp.float32)).astype(
        jnp.bfloat16
    )
    grad_x_b = passed_along(grad_tokens[None], "pipe", -1)
    return (hidden_a, grad_x_b, grad_prob[None])


MESH = pl.DeviceIdType.MESH


def ring_place(expert, n):
    z, y = lax.div(expert, 2), lax.rem(expert, 2)
    return z * (1 - y) + (n - 1 - z) * y


def ring_expert(place, n):
    place = lax.rem(place + 2 * n, n)
    back = lax.div(place, n // 2)
    return (1 - back) * (2 * place) + back * (2 * n - 1 - 2 * place)


def to_column(row):
    size = row.shape[1]
    eye = lax.broadcasted_iota(jnp.int32, (size, size), 0) == lax.broadcasted_iota(
        jnp.int32, (size, size), 1
    )
    return jnp.sum(jnp.where(eye, jnp.broadcast_to(row, (size, size)), 0.0), axis=1, keepdims=True)


def to_row(column):
    size = column.shape[0]
    eye = lax.broadcasted_iota(jnp.int32, (size, size), 0) == lax.broadcasted_iota(
        jnp.int32, (size, size), 1
    )
    return jnp.sum(
        jnp.where(eye, jnp.broadcast_to(column, (size, size)), 0.0), axis=0, keepdims=True
    )


VMEM_BYTES = 62 * 1024 * 1024 + 512 * 1024
PIECES = 4
CHUNKS = 4
PARTS = 3


def ring_kernel(
    n,
    sections,
    x_ref,
    route_a_hbm,
    prob_a_hbm,
    route_b_hbm,
    prob_b_hbm,
    wg_hbm,
    wu_hbm,
    g_hbm,
    u_hbm,
    dh_hbm,
    hidden_ref,
    gx_ref,
    gp_ref,
    route_a_ref,
    prob_a_ref,
    route_b_ref,
    prob_b_ref,
    wg,
    wu,
    g_buf,
    u_buf,
    dh_buf,
    d_gate,
    d_up,
    dx,
    rows,
    cw_in,
    ccw_in,
    cw_out,
    ccw_out,
    own_out,
    final_in,
    table_out,
    table_in,
    dp_out,
    dp_in,
    load_sem,
    small_send,
    small_recv,
    first_send,
    own_recv,
    fwd_send,
    ag_recv,
    rs_send,
    rs_recv,
    own_send,
    final_recv,
):
    tok = x_ref.shape[0]
    width = x_ref.shape[1]
    units = wg.shape[1]
    sec = lax.axis_index("pipe")
    me = lax.axis_index("expert")
    here = ring_place(me, n)
    after = lax.rem(sec + 1, sections)
    before = lax.rem(sec + sections - 1, sections)
    right = ring_expert(here + 1, n)
    left = ring_expert(here + n - 1, n)
    half = n // 2

    loads = [
        pltpu.make_async_copy(src, dst, load_sem.at[i])
        for i, (src, dst) in enumerate(
            (
                (route_a_hbm, route_a_ref),
                (prob_a_hbm, prob_a_ref),
                (route_b_hbm, route_b_ref),
                (prob_b_hbm, prob_b_ref),
                (g_hbm, g_buf),
                (u_hbm, u_buf),
                (dh_hbm, dh_buf),
                (wg_hbm, wg),
                (wu_hbm, wu),
            )
        )
    ]
    for load in loads:
        load.start()

    barrier = pltpu.get_barrier_semaphore()
    peers = [(sec, lax.rem(me + r, n)) for r in range(1, n)]
    peers += [(s, e) for s in (after, before) for e in (me, left, right)]
    for peer in peers:
        pl.semaphore_signal(barrier, inc=1, device_id=peer, device_id_type=MESH)
    pl.semaphore_wait(barrier, len(peers))

    started = []

    def send(src, dst, send_sem, recv_sem, device):
        copy = pltpu.make_async_remote_copy(
            src_ref=src,
            dst_ref=dst,
            send_sem=send_sem,
            recv_sem=recv_sem,
            device_id=device,
            device_id_type=MESH,
        )
        copy.start()
        started.append(copy)

    def arrived(dst, recv_sem):
        pltpu.make_async_remote_copy(
            src_ref=dst,
            dst_ref=dst,
            send_sem=recv_sem,
            recv_sem=recv_sem,
            device_id=(sec, right),
            device_id_type=MESH,
        ).wait_recv()

    piece = width // PIECES
    chunk = width // CHUNKS

    for c in range(PIECES):
        cols = pl.ds(c * piece, piece)
        src = x_ref.at[:, cols]
        dst = rows.at[me, :, cols]
        send(src, dst, first_send.at[0, c], ag_recv.at[0, 0, c], (after, right))
        send(src, dst, first_send.at[1, c], ag_recv.at[1, 0, c], (after, left))
    send(x_ref, rows.at[me], first_send.at[2, 0], own_recv, (after, me))

    def gather_step(d, c):
        cols = pl.ds(c * piece, piece)
        for way, step, onward in ((0, -d, right), (1, d, left)):
            if d == half and (c < PIECES // 2) != (way == 0):
                continue
            block = rows.at[ring_expert(here + step + n, n), :, cols]
            arrived(block, ag_recv.at[way, d - 1, c])
            if d < half - 1 or (d == half - 1 and (c < PIECES // 2) == (way == 0)):
                send(block, block, fwd_send.at[way, d - 1, c], ag_recv.at[way, d, c], (sec, onward))

    for load in loads[:4]:
        load.wait()
    route_a = route_a_ref[...]
    prob_a = prob_a_ref[...]
    table_out[...] = jnp.zeros_like(table_out)
    dp_out[...] = jnp.zeros_like(dp_out)
    for e in range(n):
        row = jnp.sum(jnp.where(route_a == e, prob_a, 0), axis=0, keepdims=True)
        row = row.astype(jnp.float32) / 256.0
        table_out[e, :, pl.ds(0, tok)] = jnp.broadcast_to(row, (table_out.shape[1], tok))
    for r in range(1, n):
        there = lax.rem(me - r + n, n)
        send(table_out.at[there], table_in.at[me], small_send.at[0, r], small_recv.at[0, r], (sec, there))
    table_in[me] = table_out[me]

    for load in loads[4:7]:
        load.wait()
    for j in range(n):
        span = pl.ds(j * tok, tok)
        g_val = g_buf[span, :].astype(jnp.float32)
        u_val = u_buf[span, :].astype(jnp.float32)
        dh_val = dh_buf[span, :].astype(jnp.float32)
        p_val = to_column(prob_b_ref[pl.ds(j, 1), :].astype(jnp.float32))
        sigma = jax.nn.sigmoid(g_val)
        active = g_val * sigma
        scaled = dh_val * p_val
        d_up[span, :] = (scaled * active).astype(jnp.bfloat16)
        d_gate[span, :] = (scaled * u_val * sigma * (1.0 + g_val * (1.0 - sigma))).astype(
            jnp.bfloat16
        )
        row = to_row(jnp.sum(dh_val * active * u_val, axis=1, keepdims=True))
        dp_out[j, :, pl.ds(0, tok)] = jnp.broadcast_to(row, (dp_out.shape[1], tok))
    for r in range(1, n):
        there = lax.rem(me - r + n, n)
        send(dp_out.at[there], dp_in.at[me], small_send.at[1, r], small_recv.at[1, r], (sec, there))
    dp_in[me] = dp_out[me]
    for load in loads[7:]:
        load.wait()

    contract = (((1,), (1,)), ((), ()))

    def gradient(c):
        wide = pl.ds(c * chunk, chunk)
        out = lax.dot_general(
            d_gate[...], wg[wide, :], contract, preferred_element_type=jnp.float32
        ) + lax.dot_general(d_up[...], wu[wide, :], contract, preferred_element_type=jnp.float32)
        dx[c] = out.reshape(n, tok, chunk)

    def reduce_step(c, t):
        away = half + 1 - t
        for way, step, onward, inbox, outbox in (
            (0, away, right, cw_in, cw_out),
            (1, -away, left, ccw_in, ccw_out),
        ):
            long_way = (c < CHUNKS // 2) == (way == 0)
            if t == 1 and not long_way:
                continue
            total = dx[c, ring_expert(here + step + n, n)]
            if t > 2 or (t == 2 and long_way):
                arrived(inbox.at[t - 2, c], rs_recv.at[way, t - 2, c])
                total = total + inbox[t - 2, c].astype(jnp.float32)
            outbox[t - 1, c] = total.astype(jnp.bfloat16)
            if t < half:
                send(
                    outbox.at[t - 1, c],
                    inbox.at[t - 1, c],
                    rs_send.at[way, t - 1, c],
                    rs_recv.at[way, t - 1, c],
                    (sec, onward),
                )
            else:
                send(
                    outbox.at[t - 1, c],
                    final_in.at[way, c],
                    rs_send.at[way, t - 1, c],
                    final_recv.at[way, c],
                    (before, onward),
                )

    def own_step(c):
        own_out[c] = dx[c, me].astype(jnp.bfloat16)
        send(own_out.at[c], final_in.at[2, c], own_send.at[c], final_recv.at[2, c], (before, me))

    def hidden_part(k):
        part = units // PARTS
        cols = pl.ds(k * part, part)
        tokens = rows[...].reshape(n * tok, width)
        gate = jnp.dot(tokens, wg[:, cols], preferred_element_type=jnp.float32)
        up = jnp.dot(tokens, wu[:, cols], preferred_element_type=jnp.float32)
        scale = jnp.concatenate(
            [to_column(table_in[j, 0:1, 0:tok]) for j in range(n)], axis=0
        )
        hidden_ref[:, cols] = (scale * jax.nn.silu(gate) * up).astype(jnp.bfloat16)

    gradient(0)
    own_step(0)
    reduce_step(0, 1)
    gather_step(1, 0)
    gather_step(1, 1)
    gather_step(1, 2)
    gather_step(1, 3)
    gradient(1)
    own_step(1)
    reduce_step(1, 1)
    gradient(2)
    own_step(2)
    reduce_step(2, 1)
    gradient(3)
    own_step(3)
    reduce_step(3, 1)
    gather_step(2, 0)
    gather_step(2, 1)
    gather_step(2, 2)
    gather_step(2, 3)
    reduce_step(0, 2)
    reduce_step(1, 2)
    reduce_step(2, 2)
    reduce_step(3, 2)
    gather_step(3, 0)
    gather_step(3, 1)
    gather_step(3, 2)
    gather_step(3, 3)
    reduce_step(0, 3)
    reduce_step(1, 3)
    reduce_step(2, 3)
    reduce_step(3, 3)
    reduce_step(0, 4)
    reduce_step(1, 4)
    reduce_step(2, 4)
    reduce_step(3, 4)
    gather_step(4, 0)
    gather_step(4, 1)
    gather_step(4, 2)
    gather_step(4, 3)
    arrived(rows.at[me], own_recv)
    for r in range(1, n):
        there = lax.rem(me + r, n)
        arrived(table_in.at[there], small_recv.at[0, r])
        arrived(dp_in.at[there], small_recv.at[1, r])
    hidden_part(0)
    hidden_part(1)
    hidden_part(2)
    route_b = route_b_ref[...]
    picked = jnp.zeros(route_b.shape, jnp.float32)
    for e in range(n):
        picked = picked + jnp.where(route_b == e, dp_in[e, :, 0:tok], 0.0)
    gp_ref[...] = picked.astype(jnp.bfloat16)
    for c in range(CHUNKS):
        for i in range(3):
            arrived(final_in.at[i, c], final_recv.at[i, c])
        gx_ref[:, pl.ds(c * chunk, chunk)] = (
            final_in[0, c].astype(jnp.float32)
            + final_in[1, c].astype(jnp.float32)
            + final_in[2, c].astype(jnp.float32)
        ).astype(jnp.bfloat16)
    for copy in started:
        copy.wait_send()


def put_kernel(a_ref, b_ref, c_ref, a_out, b_out, c_out, sem):
    held = ((a_ref, a_out), (b_ref, b_out), (c_ref, c_out))
    puts = [pltpu.make_async_copy(src, dst, sem.at[i]) for i, (src, dst) in enumerate(held)]
    for put in puts:
        put.start()
    for put in puts:
        put.wait()


def full_routing(
    x_prev_a,
    route_a,
    prob_a,
    w_gate,
    w_up,
    route_b,
    prob_b,
    saved_gate_b,
    saved_up_b,
    grad_hidden_b,
):
    n = lax.axis_size("expert")
    sections = lax.axis_size("pipe")
    tok, width = x_prev_a.shape[1:]
    top_k = route_a.shape[2]
    units = saved_gate_b.shape[4]
    slots = n * tok
    half = n // 2
    chunk = width // CHUNKS
    bf16, f32 = jnp.bfloat16, jnp.float32
    dma = pltpu.SemaphoreType.DMA
    vmem = pl.BlockSpec(memory_space=pltpu.VMEM)
    any_ = pl.BlockSpec(memory_space=pl.ANY)
    lanes = 128 * pl.cdiv(tok, 128)
    hidden, grad_x, grad_prob = pl.pallas_call(
        functools.partial(ring_kernel, n, sections),
        out_shape=(
            pltpu.VMEM((slots, units), bf16),
            pltpu.VMEM((tok, width), bf16),
            pltpu.VMEM((top_k, tok), bf16),
        ),
        in_specs=[any_] * 10,
        out_specs=(vmem, vmem, vmem),
        scratch_shapes=[
            pltpu.VMEM((top_k, tok), jnp.int32),
            pltpu.VMEM((top_k, tok), jnp.int32),
            pltpu.VMEM((top_k, tok), jnp.int32),
            pltpu.VMEM((n, tok), bf16),
            pltpu.VMEM((width, units), bf16),
            pltpu.VMEM((width, units), bf16),
            pltpu.VMEM((slots, units), bf16),
            pltpu.VMEM((slots, units), bf16),
            pltpu.VMEM((slots, units), bf16),
            pltpu.VMEM((slots, units), bf16),
            pltpu.VMEM((slots, units), bf16),
            pltpu.VMEM((CHUNKS, n, tok, chunk), f32),
            pltpu.VMEM((n, tok, width), bf16),
            pltpu.VMEM((half - 1, CHUNKS, tok, chunk), bf16),
            pltpu.VMEM((half - 1, CHUNKS, tok, chunk), bf16),
            pltpu.VMEM((half, CHUNKS, tok, chunk), bf16),
            pltpu.VMEM((half, CHUNKS, tok, chunk), bf16),
            pltpu.VMEM((CHUNKS, tok, chunk), bf16),
            pltpu.VMEM((3, CHUNKS, tok, chunk), bf16),
            pltpu.VMEM((n, top_k, lanes), f32),
            pltpu.VMEM((n, top_k, lanes), f32),
            pltpu.VMEM((n, top_k, lanes), f32),
            pltpu.VMEM((n, top_k, lanes), f32),
            dma((9,)),
            dma((2, n)),
            dma((2, n)),
            dma((3, PIECES)),
            dma,
            dma((2, half, PIECES)),
            dma((2, half, PIECES)),
            dma((2, half, CHUNKS)),
            dma((2, half, CHUNKS)),
            dma((CHUNKS,)),
            dma((3, CHUNKS)),
        ],
        compiler_params=pltpu.CompilerParams(
            collective_id=0, has_side_effects=True, vmem_limit_bytes=VMEM_BYTES
        ),
        name="ring",
    )(
        x_prev_a[0],
        route_a[0].T,
        prob_a[0].T,
        route_b[0].T,
        prob_b[0, 0],
        w_gate[0],
        w_up[0],
        saved_gate_b.reshape(slots, units),
        saved_up_b.reshape(slots, units),
        grad_hidden_b.reshape(slots, units),
    )
    results = (hidden, grad_x, grad_prob)
    hidden, grad_x, grad_prob = pl.pallas_call(
        put_kernel,
        out_shape=tuple(jax.ShapeDtypeStruct(a.shape, a.dtype) for a in results),
        in_specs=[any_] * 3,
        out_specs=(any_,) * 3,
        scratch_shapes=[dma((3,))],
        compiler_params=pltpu.CompilerParams(vmem_limit_bytes=1 << 20),
        name="put",
    )(*results)
    return (
        hidden.reshape(1, 1, n, tok, units),
        grad_x[None],
        grad_prob.T[None],
    )


def any_routing(*args):
    tokens, top_k = args[1].shape[1:]
    capacity = args[7].shape[3]
    full = top_k == lax.axis_size("expert") and capacity == tokens
    if full and top_k == 8 and lax.axis_size("pipe") > 2:
        return full_routing(*args)
    return per_device(*args)


def solution(mesh):
    return jax.shard_map(
        any_routing,
        mesh=mesh,
        in_specs=(
            P("pipe", "expert", None),
            P("pipe", "expert", None),
            P("pipe", "expert", None),
            P("expert", None, None),
            P("expert", None, None),
            P("pipe", "expert", None),
            P("pipe", "expert", None, None),
            P("pipe", "expert", None, None, None),
            P("pipe", "expert", None, None, None),
            P("pipe", "expert", None, None, None),
        ),
        out_specs=(
            P("pipe", "expert", None, None, None),
            P("pipe", "expert", None),
            P("pipe", "expert", None),
        ),
        check_vma=False,
    )
```

```python
import functools

import jax
import jax.numpy as jnp
from jax import lax
from jax.experimental import pallas as pl
from jax.experimental.pallas import tpu as pltpu
from jax.sharding import PartitionSpec as P


def passed_along(block, axis, distance):
    devices = range(lax.axis_size(axis))
    route = [((i - distance) % len(devices), i) for i in devices]
    return lax.ppermute(block, axis, route)


def slot_choice(route, capacity, experts):
    expert_ids = route[0]
    tok_rows, top_k = expert_ids.shape
    flat_ids = expert_ids.reshape(-1)
    onehot = (flat_ids[:, None] == jnp.arange(experts, dtype=jnp.int32)[None, :]).astype(jnp.int32)
    rows = flat_ids.shape[0]
    earlier = jnp.arange(rows)[:, None] > jnp.arange(rows)[None, :]
    before = jnp.dot(
        earlier.astype(jnp.bfloat16),
        onehot.astype(jnp.bfloat16),
        preferred_element_type=jnp.float32,
    ).astype(jnp.int32)
    slot_rank = jnp.sum(before * onehot, axis=1)
    target = jnp.where(slot_rank < capacity, flat_ids * capacity + slot_rank, -1).reshape(
        tok_rows, top_k
    )
    slot_ids = jnp.arange(experts * capacity, dtype=jnp.int32)
    return (target[:, :, None] == slot_ids[None, None, :]).astype(jnp.float32)


def dispatch_rows(tokens, route, quant, capacity, experts):
    chosen = slot_choice(route, capacity, experts)
    picker = jnp.sum(chosen, axis=1).astype(jnp.bfloat16)
    send_x = jnp.einsum("ts,td->sd", picker, tokens[0], preferred_element_type=jnp.float32).astype(
        jnp.bfloat16
    )
    send_p = (jnp.einsum("tks,tk->s", chosen, quant[0].astype(jnp.float32)) / 256.0).astype(
        jnp.bfloat16
    )
    return (send_x.reshape(experts, capacity, -1), send_p.reshape(experts, capacity))


def per_device(
    x_prev_a,
    route_a,
    prob_a,
    w_gate,
    w_up,
    route_b,
    prob_b,
    saved_gate_b,
    saved_up_b,
    grad_hidden_b,
):
    experts = lax.axis_size("expert")
    capacity = saved_gate_b.shape[3]
    width = x_prev_a.shape[2]
    units = saved_gate_b.shape[4]
    gate_weight = w_gate[0]
    up_weight = w_up[0]
    x_here = passed_along(x_prev_a, "pipe", 1)
    send_x, send_p = dispatch_rows(x_here, route_a, prob_a, capacity, experts)
    recv_x, recv_p = (
        lax.all_to_all(send_x, "expert", split_axis=0, concat_axis=0, tiled=True),
        lax.all_to_all(send_p, "expert", split_axis=0, concat_axis=0, tiled=True),
    )
    rows = recv_x.reshape(-1, width)
    gate = jnp.dot(rows, gate_weight, preferred_element_type=jnp.float32)
    up_proj = jnp.dot(rows, up_weight, preferred_element_type=jnp.float32)
    scale = recv_p.reshape(-1, 1).astype(jnp.float32)
    hidden = (scale * jax.nn.silu(gate) * up_proj).astype(jnp.bfloat16)
    hidden_a = hidden.reshape(1, 1, experts, capacity, units)
    g_val = saved_gate_b[0, 0].reshape(-1, units).astype(jnp.float32)
    u_val = saved_up_b[0, 0].reshape(-1, units).astype(jnp.float32)
    dh_val = grad_hidden_b[0, 0].reshape(-1, units).astype(jnp.float32)
    p_val = prob_b[0, 0].reshape(-1, 1).astype(jnp.float32)
    sigma = jax.nn.sigmoid(g_val)
    active = g_val * sigma
    scaled = dh_val * p_val
    d_up = (scaled * active).astype(jnp.bfloat16)
    d_gate = (scaled * u_val * sigma * (1.0 + g_val * (1.0 - sigma))).astype(jnp.bfloat16)
    slot_dx = (
        jnp.einsum("rh,dh->rd", d_gate, gate_weight, preferred_element_type=jnp.float32)
        + jnp.einsum("rh,dh->rd", d_up, up_weight, preferred_element_type=jnp.float32)
    ).astype(jnp.bfloat16)
    slot_dp = jnp.sum(dh_val * active * u_val, axis=1).astype(jnp.bfloat16)
    back_x, back_p = (
        lax.all_to_all(
            slot_dx.reshape(experts, capacity, width),
            "expert",
            split_axis=0,
            concat_axis=0,
            tiled=True,
        ),
        lax.all_to_all(
            slot_dp.reshape(experts, capacity), "expert", split_axis=0, concat_axis=0, tiled=True
        ),
    )
    chosen_b = slot_choice(route_b, capacity, experts)
    picker_b = jnp.sum(chosen_b, axis=1).astype(jnp.bfloat16)
    grad_tokens = jnp.dot(
        picker_b, back_x.reshape(-1, width), preferred_element_type=jnp.float32
    ).astype(jnp.bfloat16)
    grad_prob = jnp.einsum("tks,s->tk", chosen_b, back_p.reshape(-1).astype(jnp.float32)).astype(
        jnp.bfloat16
    )
    grad_x_b = passed_along(grad_tokens[None], "pipe", -1)
    return (hidden_a, grad_x_b, grad_prob[None])


MESH = pl.DeviceIdType.MESH


def to_column(row):
    size = row.shape[1]
    eye = lax.broadcasted_iota(jnp.int32, (size, size), 0) == lax.broadcasted_iota(
        jnp.int32, (size, size), 1
    )
    return jnp.sum(jnp.where(eye, jnp.broadcast_to(row, (size, size)), 0.0), axis=1, keepdims=True)


VMEM_BYTES = 62 * 1024 * 1024 + 512 * 1024
LANES = 128
ROWS_Y = 2
PARTS = 3


SHARES = ((6, True), (6, True), (2, False), (2, False))


def pieces_of(width):
    units, whole = width // LANES, sum(share for share, _ in SHARES)
    pieces, start, taken = [], 0, 0
    for share, z_first in SHARES:
        taken += share
        end = units * taken // whole
        pieces.append((start * LANES, (end - start) * LANES, z_first))
        start = end
    begin, size, z_first = pieces[-1]
    pieces[-1] = (begin, size + LANES, z_first)
    return pieces


COMPUTE = ((0, 0), (0, 1), (0, 2), (0, 3), (1, 0), (1, 1), (1, 2), (1, 3), (2, 0), (2, 1))
ORDERS = (
    (
        (),
        (),
        (),
        (),
        (),
        ((1, 0, 3),),
        ((1, 1, 3),),
        ((1, 1, 2), (2, 2, 3), (1, 0, 2)),
        ((2, 3, 3), (1, 1, 0), (2, 2, 2), (1, 0, 0), (1, 1, 1), (1, 0, 1), (2, 3, 2), (2, 2, 1), (2, 3, 1), (0, 0, 0, 0), (0, 1, 0, 0), (0, 3, 0, 0), (0, 0, 1, 0), (0, 2, 0, 0), (0, 1, 1, 0), (0, 0, 0, 1), (0, 3, 1, 0), (0, 2, 1, 0), (0, 1, 0, 1), (2, 0, 3), (0, 3, 0, 1), (0, 2, 0, 1), (2, 1, 3), (2, 1, 2), (2, 0, 2), (0, 0, 0, 2), (0, 3, 1, 1), (0, 1, 0, 2), (0, 2, 1, 1), (0, 3, 0, 2), (0, 2, 0, 2), (4, 1), (2, 1, 1), (4, 0), (2, 0, 1), (0, 0, 0, 3), (0, 1, 0, 3), (0, 3, 0, 3), (0, 2, 0, 3), (0, 0, 1, 1), (0, 3, 1, 2), (0, 2, 1, 2), (0, 1, 1, 1)),
        ((4, 3), (0, 0, 1, 2), (4, 2), (0, 1, 1, 2), (0, 3, 1, 3), (0, 0, 1, 3), (0, 2, 1, 3), (0, 1, 1, 3)),
        (),
    ),
    (
        (),
        (),
        (),
        (),
        (),
        ((1, 0, 3),),
        ((1, 1, 3), (1, 0, 0), (1, 1, 0)),
        ((1, 1, 1), (1, 1, 2), (1, 0, 1), (1, 0, 2)),
        ((0, 0, 0, 1), (0, 0, 0, 0), (0, 1, 0, 1), (0, 0, 1, 1), (0, 3, 0, 1), (0, 1, 0, 0), (0, 2, 0, 1), (0, 3, 0, 0), (0, 0, 0, 2), (0, 1, 1, 1), (0, 2, 0, 0), (0, 3, 1, 1), (0, 1, 0, 2), (0, 2, 1, 1), (2, 2, 3), (0, 3, 0, 2), (0, 2, 0, 2), (2, 3, 3), (2, 2, 2), (2, 3, 2), (0, 0, 0, 3), (0, 1, 0, 3), (0, 3, 0, 3), (0, 2, 0, 3), (0, 3, 1, 2), (0, 3, 1, 0), (0, 2, 1, 2), (0, 2, 1, 0), (2, 0, 3), (3, 3, 0), (4, 1), (2, 1, 3), (3, 2, 0), (4, 3), (4, 0), (2, 1, 2), (4, 2), (2, 0, 2), (0, 3, 1, 3), (0, 2, 1, 3), (0, 0, 1, 0), (3, 0, 0), (0, 1, 1, 0)),
        ((3, 1, 0), (0, 0, 1, 2), (0, 1, 1, 2), (0, 0, 1, 3), (0, 1, 1, 3)),
        (),
    ),
    (
        (),
        (),
        (),
        (),
        (),
        ((1, 0, 0),),
        ((1, 1, 0),),
        (),
        ((1, 1, 1), (1, 0, 1), (1, 1, 2), (1, 0, 2), (1, 1, 3), (1, 0, 3), (0, 0, 0, 2), (0, 1, 0, 2), (0, 0, 0, 1), (0, 0, 0, 3), (0, 0, 1, 2), (0, 3, 0, 2), (0, 2, 0, 2), (0, 1, 0, 3), (0, 1, 0, 1), (0, 1, 1, 2), (0, 3, 0, 3), (0, 2, 0, 3), (0, 3, 0, 1), (0, 3, 1, 2), (0, 2, 0, 1), (0, 2, 1, 2), (3, 3, 0), (0, 0, 0, 0), (3, 2, 0), (3, 3, 1), (0, 1, 0, 0), (0, 3, 0, 0), (0, 2, 0, 0), (3, 2, 1), (0, 3, 1, 1), (2, 2, 3), (0, 2, 1, 1), (0, 3, 1, 3), (0, 2, 1, 3), (2, 3, 3), (4, 2), (3, 0, 0), (4, 1), (4, 3), (4, 0), (3, 1, 0), (0, 3, 1, 0), (0, 2, 1, 0), (3, 1, 1), (2, 0, 3), (3, 0, 1), (0, 0, 1, 1), (0, 0, 1, 3), (2, 1, 3), (0, 1, 1, 1), (0, 1, 1, 3)),
        ((0, 0, 1, 0), (0, 1, 1, 0)),
        (),
    ),
    (
        (),
        (),
        (),
        (),
        (),
        ((1, 0, 0),),
        ((1, 1, 0),),
        (),
        ((1, 1, 1), (1, 0, 1), (3, 3, 0), (3, 2, 0), (3, 3, 1), (1, 1, 2), (1, 0, 2), (3, 2, 1), (1, 1, 3), (3, 3, 2), (1, 0, 3), (3, 2, 2), (0, 0, 0, 3), (0, 1, 0, 3), (0, 0, 1, 3), (0, 0, 0, 2), (0, 3, 0, 3), (0, 1, 1, 3), (0, 2, 0, 3), (0, 3, 1, 3), (0, 1, 0, 2), (0, 2, 1, 3), (0, 3, 0, 2), (0, 2, 0, 2), (3, 0, 0), (3, 1, 0), (0, 0, 0, 1), (0, 1, 0, 1), (3, 1, 1), (0, 3, 0, 1), (3, 0, 1), (0, 3, 1, 2), (0, 2, 0, 1), (0, 2, 1, 2), (3, 1, 2), (3, 0, 2), (0, 0, 0, 0), (4, 1), (0, 1, 0, 0), (0, 3, 0, 0), (4, 0), (0, 2, 0, 0), (0, 3, 1, 1), (4, 2), (0, 2, 1, 1), (0, 0, 1, 2), (0, 1, 1, 2)),
        ((4, 3), (0, 3, 1, 0), (0, 0, 1, 1), (0, 2, 1, 0), (0, 1, 1, 1), (0, 0, 1, 0), (0, 1, 1, 0)),
        (),
    ),
)


def mesh_kernel(
    n,
    sections,
    x_hbm,
    route_a_hbm,
    prob_a_hbm,
    route_b_hbm,
    prob_b_hbm,
    wg_hbm,
    wu_hbm,
    g_hbm,
    u_hbm,
    dh_hbm,
    hidden_ref,
    gx_ref,
    gp_ref,
    route_a_ref,
    prob_a_ref,
    route_b_ref,
    prob_b_ref,
    wg,
    wu,
    g_buf,
    u_buf,
    dh_buf,
    d_gate,
    d_up,
    rows,
    dx,
    in_up,
    in_down,
    in_y,
    fin_in,
    load_sem,
    weight_sem,
    shift_send,
    tab_send,
    tab_recv,
    ag_send,
    ag_recv,
    up_send,
    up_recv,
    down_send,
    down_recv,
    y_send,
    y_recv,
    fin_send,
    fin_recv,
):
    tok, width = x_hbm.shape
    units = wg.shape[1]
    pieces = pieces_of(width)
    nz = n // ROWS_Y
    sec = lax.axis_index("pipe")
    me = lax.axis_index("expert")
    z, y = lax.div(me, ROWS_Y), lax.rem(me, ROWS_Y)
    after = lax.rem(sec + 1, sections)
    before = lax.rem(sec + sections - 1, sections)
    across = me + 1 - 2 * y
    top = nz - 1

    loads = [
        pltpu.make_async_copy(src, dst, load_sem.at[i])
        for i, (src, dst) in enumerate(
            (
                (route_a_hbm, route_a_ref),
                (prob_a_hbm, prob_a_ref),
                (route_b_hbm, route_b_ref),
                (prob_b_hbm, prob_b_ref),
                (g_hbm, g_buf),
                (u_hbm, u_buf),
                (dh_hbm, dh_buf),
            )
        )
    ]
    for load in loads:
        load.start()

    barrier = pltpu.get_barrier_semaphore()

    def greet(peer):
        pl.semaphore_signal(barrier, inc=1, device_id=peer, device_id_type=MESH)

    for peer in ((after, me), (before, me)):
        greet(peer)
    for section in (sec, after, before):
        greet((section, across))

        @pl.when(z < top)
        def _():
            greet((section, me + ROWS_Y))

        @pl.when(z > 0)
        def _():
            greet((section, me - ROWS_Y))

    def dx_rows(start, size):
        return pl.ds(start, min(start + size, width) - start)

    weights = {}
    for c in [c for what, c in COMPUTE if what == 1]:
        start, size, _ = pieces[c]
        span = dx_rows(start, size)
        weights[c] = [
            pltpu.make_async_copy(src.at[span, :], dst.at[span, :], weight_sem.at[i, c])
            for i, (src, dst) in enumerate(((wg_hbm, wg), (wu_hbm, wu)))
        ]
        for load in weights[c]:
            load.start()

    def cols(c):
        start, size, _ = pieces[c]
        return pl.ds(start, size)

    def x_cols(c):
        start, size, _ = pieces[c]
        return dx_rows(start, size)

    table_cols = pl.ds(width, LANES)
    last = len(pieces) - 1
    for load in loads[:2]:
        load.wait()
    route_a = route_a_ref[...]
    prob_a = prob_a_ref[...]
    lane = lax.broadcasted_iota(jnp.int32, (n, LANES), 1)
    expert = lax.broadcasted_iota(jnp.int32, (n, LANES), 0)
    spread = (lane == expert).astype(jnp.bfloat16)
    by_expert = jnp.concatenate(
        [jnp.sum(jnp.where(route_a == e, prob_a, 0), axis=0, keepdims=True) for e in range(n)],
        axis=0,
    )
    rows[me, :, table_cols] = lax.dot_general(
        by_expert.astype(jnp.float32).astype(jnp.bfloat16),
        spread,
        (((0,), (0,)), ((), ())),
        preferred_element_type=jnp.float32,
    ).astype(jnp.bfloat16)

    pl.semaphore_wait(
        barrier,
        5 + 3 * jnp.where(z < top, 1, 0) + 3 * jnp.where(z > 0, 1, 0),
    )

    for c in range(len(pieces)):
        if pieces[c][2]:

            @pl.when(z == 0)
            def _():
                fin_in[1, :, cols(c)] = jnp.zeros((tok, pieces[c][1]), fin_in.dtype)

            @pl.when(z == top)
            def _():
                fin_in[2, :, cols(c)] = jnp.zeros((tok, pieces[c][1]), fin_in.dtype)

    started = []

    def remote(src, dst, send_sem, recv_sem, device):
        return pltpu.make_async_remote_copy(
            src_ref=src,
            dst_ref=dst,
            send_sem=send_sem,
            recv_sem=recv_sem,
            device_id=device,
            device_id_type=MESH,
        )

    def arrived(dst, recv_sem):
        remote(dst, dst, recv_sem, recv_sem, (sec, across)).wait_recv()

    def at(zz):
        return pl.when(z == zz)

    UP, DOWN, OVER = 0, 1, 2

    def toward(way):
        return (sec, (me + ROWS_Y, me - ROWS_Y, across)[way])

    def post(zz, copy):
        remote(*copy()).start()
        started.append((zz, copy))

    def neighbours():
        yield None, OVER, across, 1
        for zz in range(nz):
            if zz < top:
                yield zz, UP, me + ROWS_Y, 0
            if zz > 0:
                yield zz, DOWN, me - ROWS_Y, 0

    def first(zz, way, there, v, c):
        def copy():
            span = table_cols if c is None else x_cols(c)
            held = rows.at[me, :, span]
            if c is None:
                return held, held, tab_send.at[way], tab_recv.at[v, z], (sec, there)
            return x_hbm.at[:, span], held, shift_send.at[c, way], ag_recv.at[c, v, z], (after, there)

        post(zz, copy)

    for c in [*range(len(pieces)), None]:
        for zz, way, there, v in neighbours():
            if zz is None:
                first(zz, way, there, v, c)
            else:

                @at(zz)
                def _():
                    first(zz, way, there, v, c)

        if c is not None:
            post(
                None,
                lambda c=c: (
                    x_hbm.at[:, x_cols(c)],
                    rows.at[me, :, x_cols(c)],
                    shift_send.at[c, 3],
                    ag_recv.at[c, 0, z],
                    (after, me),
                ),
            )

    def expert_at(zz, v):
        return ROWS_Y * zz + (y if v == 0 else 1 - y)

    def ways_of(zz, c, v, zs):
        z_first = pieces[c][2]
        ways = []
        if v == 0 and zs == zz:
            return ways
        if zs <= zz and zz < top and not (z_first and v == 1):
            ways.append(UP)
        if zs >= zz and zz > 0 and not (z_first and v == 1):
            ways.append(DOWN)
        if v == 0 and z_first:
            ways.append(OVER)
        return ways

    def spread_block(zz, c, v, zs):
        block = expert_at(zs, v)
        near_by = abs(zs - zz) <= 1 - v
        wide = x_cols(c) if near_by else cols(c)
        arrived(rows.at[block, :, wide], ag_recv.at[c, v, zs])
        if near_by and c == last and not (v == 0 and zs == zz):
            arrived(rows.at[block, :, table_cols], tab_recv.at[v, zs])
        for way in ways_of(zz, c, v, zs):

            def copy(way=way):
                held = rows.at[expert_at(zs, v), :, cols(c)]
                there = 1 if way == OVER else v
                recv = ag_recv.at[c, there, zs]
                return held, held, ag_send.at[c, v, zs, way], recv, toward(way)

            post(zz, copy)

    def backward_rows(j):
        span = pl.ds(j * tok, tok)
        g_val = g_buf[span, :].astype(jnp.float32)
        u_val = u_buf[span, :].astype(jnp.float32)
        dh_val = dh_buf[span, :].astype(jnp.float32)
        p_val = to_column(prob_b_ref[pl.ds(j, 1), :].astype(jnp.float32))
        sigma = jax.nn.sigmoid(g_val)
        active = g_val * sigma
        scaled = dh_val * p_val
        d_up[span, :] = (scaled * active).astype(jnp.bfloat16)
        d_gate[span, :] = (scaled * u_val * sigma * (1.0 + g_val * (1.0 - sigma))).astype(
            jnp.bfloat16
        )
        column = jnp.sum(dh_val * active * u_val, axis=1, keepdims=True)
        lanes = lax.broadcasted_iota(jnp.int32, (tok, LANES), 1)
        dx[j, :, table_cols] = jnp.where(lanes == me, column, 0.0).astype(jnp.bfloat16)

    contract = (((1,), (1,)), ((), ()))

    def gradient(c):
        for load in weights[c]:
            load.wait()
        span = x_cols(c)
        out = lax.dot_general(
            d_gate[...], wg[span, :], contract, preferred_element_type=jnp.float32
        ) + lax.dot_general(d_up[...], wu[span, :], contract, preferred_element_type=jnp.float32)
        dx[:, :, span] = out.reshape(n, tok, out.shape[1]).astype(jnp.bfloat16)

    def f32(ref_value):
        return ref_value.astype(jnp.float32)

    def trade(zz, c, zt):
        post(
            zz,
            lambda: (
                dx.at[expert_at(zt, 1), :, cols(c)],
                in_y.at[zt, :, cols(c)],
                y_send.at[c, zt],
                y_recv.at[c, zt],
                toward(OVER),
            ),
        )

    def pass_on(zz, c, zt, way):
        z_first = pieces[c][2]
        inbox = in_up if way == UP else in_down
        send_sem, recv_sem = (up_send, up_recv) if way == UP else (down_send, down_recv)
        begins = zz == 0 if way == UP else zz == top
        if z_first:
            here = expert_at(zt, 0)
            total = f32(dx[here, :, cols(c)])
            arrived(in_y.at[zt, :, cols(c)], y_recv.at[c, zt])
            total = total + f32(in_y[zt, :, cols(c)])
            if not begins:
                arrived(inbox.at[here, :, cols(c)], recv_sem.at[c, zt])
                total = total + f32(inbox[here, :, cols(c)])
            dx[here, :, cols(c)] = total.astype(jnp.bfloat16)
        else:
            pair = pl.ds(ROWS_Y * zt, ROWS_Y)
            if not begins:
                arrived(inbox.at[pair, :, cols(c)], recv_sem.at[c, zt])
                total = f32(dx[pair, :, cols(c)]) + f32(inbox[pair, :, cols(c)])
                dx[pair, :, cols(c)] = total.astype(jnp.bfloat16)

        def copy():
            block = expert_at(zt, 0) if z_first else pl.ds(ROWS_Y * zt, ROWS_Y)
            src, dst = dx.at[block, :, cols(c)], inbox.at[block, :, cols(c)]
            if z_first and abs(zt - zz) == 1:
                there = (before, toward(way)[1])
                return src, fin_in.at[1 + way, :, cols(c)], fin_send.at[c, 1 + way], fin_recv.at[c, 1 + way], there
            return src, dst, send_sem.at[c, zt], recv_sem.at[c, zt], toward(way)

        post(zz, copy)

    def line_total(zz, c, block):
        total = f32(dx[block, :, cols(c)])
        if zz > 0:
            total = total + f32(in_up[block, :, cols(c)])
        if zz < top:
            total = total + f32(in_down[block, :, cols(c)])
        return total

    def own_line(zz, c):
        z_first = pieces[c][2]
        own, other = expert_at(zz, 0), expert_at(zz, 1)
        if z_first:
            arrived(in_y.at[zz, :, cols(c)], y_recv.at[c, zz])
            total = f32(dx[own, :, cols(c)]) + f32(in_y[zz, :, cols(c)])
            dx[own, :, cols(c)] = total.astype(jnp.bfloat16)
        else:
            pair = pl.ds(ROWS_Y * zz, ROWS_Y)
            if zz > 0:
                arrived(in_up.at[pair, :, cols(c)], up_recv.at[c, zz])
            if zz < top:
                arrived(in_down.at[pair, :, cols(c)], down_recv.at[c, zz])
            dx[other, :, cols(c)] = line_total(zz, c, other).astype(jnp.bfloat16)
            post(
                zz,
                lambda: (
                    dx.at[expert_at(zz, 1), :, x_cols(c)],
                    fin_in.at[1, :, x_cols(c)],
                    fin_send.at[c, 1],
                    fin_recv.at[c, 1],
                    (before, across),
                ),
            )
            if c == last:
                post(
                    zz,
                    lambda: (
                        dx.at[expert_at(zz, 1), :, table_cols],
                        in_y.at[zz, :, table_cols],
                        y_send.at[c, zz],
                        y_recv.at[c, zz],
                        toward(OVER),
                    ),
                )
            dx[own, :, cols(c)] = line_total(zz, c, own).astype(jnp.bfloat16)
        post(
            zz,
            lambda: (
                dx.at[expert_at(zz, 0), :, x_cols(c)],
                fin_in.at[0, :, x_cols(c)],
                fin_send.at[c, 0],
                fin_recv.at[c, 0],
                (before, me),
            ),
        )

    group = n // 2
    near = lax.div(z, nz // 2)

    def hidden_part(half, k):
        part = units // PARTS
        span = pl.ds(k * part, part)
        blocks = pl.ds(half * group, group)
        tokens = rows[blocks, :, pl.ds(0, width)].reshape(group * tok, width)
        gate = jnp.dot(tokens, wg[:, span], preferred_element_type=jnp.float32)
        up = jnp.dot(tokens, wu[:, span], preferred_element_type=jnp.float32)
        table = rows[blocks, :, table_cols].reshape(group * tok, LANES).astype(jnp.float32)
        lanes = lax.broadcasted_iota(jnp.int32, table.shape, 1)
        scale = jnp.sum(jnp.where(lanes == me, table, 0.0), axis=1, keepdims=True) / 256.0
        lines = pl.ds(pl.multiple_of(half * (group * tok), group * tok), group * tok)
        hidden_ref[lines, span] = (scale * jax.nn.silu(gate) * up).astype(jnp.bfloat16)

    def load_saved():
        for load in loads[3:]:
            load.wait()

    def pick():
        loads[2].wait()
        arrived(in_y.at[z, :, table_cols], y_recv.at[last, z])
        table = f32(dx[me, :, table_cols]) + f32(in_y[z, :, table_cols])
        table = table.astype(jnp.bfloat16)
        by_slot = lax.dot_general(
            spread, table, (((1,), (1,)), ((), ())), preferred_element_type=jnp.float32
        )
        route_b = route_b_ref[...]
        picked = jnp.zeros(route_b.shape, jnp.float32)
        for e in range(n):
            picked = picked + jnp.where(route_b == e, by_slot[e : e + 1, :], 0.0)
        gp_ref[...] = picked.astype(jnp.bfloat16)

    def step(zz, what, c, *rest):
        if what == 0:
            spread_block(zz, c, *rest)
        elif what == 1:
            trade(zz, c, *rest)
        elif what == 4:
            own_line(zz, c)
        else:
            pass_on(zz, c, *rest, UP if what == 2 else DOWN)

    def work(what, k):
        share = n // sum(1 for kind, _ in COMPUTE if kind == 0)
        if what == 0:
            if k == 0:
                load_saved()
            for j in range(k * share, (k + 1) * share):
                backward_rows(j)
        elif what == 1:
            gradient(k)
        else:
            for part in range(PARTS):
                hidden_part(near if k == 0 else 1 - near, part)

    for i in range(len(COMPUTE) + 1):
        for zz in range(nz):
            if ORDERS[zz][i]:

                @at(zz)
                def _():
                    for each in ORDERS[zz][i]:
                        step(zz, *each)

        if i < len(COMPUTE):
            work(*COMPUTE[i])

    pick()
    for c in range(len(pieces)):
        span = x_cols(c)
        arrived(fin_in.at[0, :, span], fin_recv.at[c, 0])
        if pieces[c][2]:

            @pl.when(z > 0)
            def _():
                arrived(fin_in.at[1, :, span], fin_recv.at[c, 1])

            @pl.when(z < top)
            def _():
                arrived(fin_in.at[2, :, span], fin_recv.at[c, 2])

            total = f32(fin_in[0, :, span]) + f32(fin_in[1, :, span]) + f32(fin_in[2, :, span])
        else:
            arrived(fin_in.at[1, :, span], fin_recv.at[c, 1])
            total = f32(fin_in[0, :, span]) + f32(fin_in[1, :, span])
        gx_ref[:, span] = total.astype(jnp.bfloat16)
    for zz in [None, *range(nz)]:
        copies = [copy for where, copy in started if where == zz]
        if zz is None:
            for copy in copies:
                remote(*copy()).wait_send()
        else:

            @at(zz)
            def _():
                for copy in copies:
                    remote(*copy()).wait_send()


def put_kernel(a_ref, b_ref, c_ref, a_out, b_out, c_out, sem):
    held = ((a_ref, a_out), (b_ref, b_out), (c_ref, c_out))
    puts = [pltpu.make_async_copy(src, dst, sem.at[i]) for i, (src, dst) in enumerate(held)]
    for put in puts:
        put.start()
    for put in puts:
        put.wait()


def full_routing(
    x_prev_a,
    route_a,
    prob_a,
    w_gate,
    w_up,
    route_b,
    prob_b,
    saved_gate_b,
    saved_up_b,
    grad_hidden_b,
):
    n = lax.axis_size("expert")
    sections = lax.axis_size("pipe")
    tok, width = x_prev_a.shape[1:]
    top_k = route_a.shape[2]
    units = saved_gate_b.shape[4]
    slots = n * tok
    nz = n // ROWS_Y
    count = len(pieces_of(width))
    wide = width + LANES
    bf16 = jnp.bfloat16
    dma = pltpu.SemaphoreType.DMA
    any_ = pl.BlockSpec(memory_space=pl.ANY)
    vmem = pl.BlockSpec(memory_space=pltpu.VMEM)
    hidden, grad_x, grad_prob = pl.pallas_call(
        functools.partial(mesh_kernel, n, sections),
        out_shape=(
            pltpu.VMEM((slots, units), bf16),
            pltpu.VMEM((tok, width), bf16),
            pltpu.VMEM((top_k, tok), bf16),
        ),
        in_specs=[any_] * 10,
        out_specs=(vmem,) * 3,
        scratch_shapes=[
            pltpu.VMEM((top_k, tok), jnp.int32),
            pltpu.VMEM((top_k, tok), jnp.int32),
            pltpu.VMEM((top_k, tok), jnp.int32),
            pltpu.VMEM((n, tok), bf16),
            pltpu.VMEM((width, units), bf16),
            pltpu.VMEM((width, units), bf16),
            pltpu.VMEM((slots, units), bf16),
            pltpu.VMEM((slots, units), bf16),
            pltpu.VMEM((slots, units), bf16),
            pltpu.VMEM((slots, units), bf16),
            pltpu.VMEM((slots, units), bf16),
            pltpu.VMEM((n, tok, wide), bf16),
            pltpu.VMEM((n, tok, wide), bf16),
            pltpu.VMEM((n, tok, wide), bf16),
            pltpu.VMEM((n, tok, wide), bf16),
            pltpu.VMEM((nz, tok, wide), bf16),
            pltpu.VMEM((3, tok, wide), bf16),
            dma((7,)),
            dma((2, count)),
            dma((count, 4)),
            dma((3,)),
            dma((2, nz)),
            dma((count, 2, nz, 3)),
            dma((count, 2, nz)),
            dma((count, nz)),
            dma((count, nz)),
            dma((count, nz)),
            dma((count, nz)),
            dma((count, nz)),
            dma((count, nz)),
            dma((count, 3)),
            dma((count, 3)),
        ],
        compiler_params=pltpu.CompilerParams(
            collective_id=0, has_side_effects=True, vmem_limit_bytes=VMEM_BYTES
        ),
        name="mesh",
    )(
        x_prev_a[0],
        route_a[0].T,
        prob_a[0].T,
        route_b[0].T,
        prob_b[0, 0],
        w_gate[0],
        w_up[0],
        saved_gate_b.reshape(slots, units),
        saved_up_b.reshape(slots, units),
        grad_hidden_b.reshape(slots, units),
    )
    results = (hidden, grad_x, grad_prob)
    hidden, grad_x, grad_prob = pl.pallas_call(
        put_kernel,
        out_shape=tuple(jax.ShapeDtypeStruct(a.shape, a.dtype) for a in results),
        in_specs=[any_] * 3,
        out_specs=(any_,) * 3,
        scratch_shapes=[dma((3,))],
        compiler_params=pltpu.CompilerParams(vmem_limit_bytes=1 << 20),
        name="put",
    )(*results)
    return (
        hidden.reshape(1, 1, n, tok, units),
        grad_x[None],
        grad_prob.T[None],
    )


def any_routing(*args):
    tokens, top_k = args[1].shape[1:]
    capacity = args[7].shape[3]
    full = top_k == lax.axis_size("expert") and capacity == tokens
    if full and top_k == 8 == ROWS_Y * len(ORDERS) and lax.axis_size("pipe") > 2:
        return full_routing(*args)
    return per_device(*args)


def solution(mesh):
    return jax.shard_map(
        any_routing,
        mesh=mesh,
        in_specs=(
            P("pipe", "expert", None),
            P("pipe", "expert", None),
            P("pipe", "expert", None),
            P("expert", None, None),
            P("expert", None, None),
            P("pipe", "expert", None),
            P("pipe", "expert", None, None),
            P("pipe", "expert", None, None, None),
            P("pipe", "expert", None, None, None),
            P("pipe", "expert", None, None, None),
        ),
        out_specs=(
            P("pipe", "expert", None, None, None),
            P("pipe", "expert", None),
            P("pipe", "expert", None),
        ),
        check_vma=False,
    )
```

```python
import functools

import jax
import jax.numpy as jnp
from jax import lax
from jax.experimental import pallas as pl
from jax.experimental.pallas import tpu as pltpu
from jax.sharding import PartitionSpec as P


def passed_along(block, axis, distance):
    devices = range(lax.axis_size(axis))
    route = [((i - distance) % len(devices), i) for i in devices]
    return lax.ppermute(block, axis, route)


def slot_choice(route, capacity, experts):
    expert_ids = route[0]
    tok_rows, top_k = expert_ids.shape
    flat_ids = expert_ids.reshape(-1)
    onehot = (flat_ids[:, None] == jnp.arange(experts, dtype=jnp.int32)[None, :]).astype(jnp.int32)
    rows = flat_ids.shape[0]
    earlier = jnp.arange(rows)[:, None] > jnp.arange(rows)[None, :]
    before = jnp.dot(
        earlier.astype(jnp.bfloat16),
        onehot.astype(jnp.bfloat16),
        preferred_element_type=jnp.float32,
    ).astype(jnp.int32)
    slot_rank = jnp.sum(before * onehot, axis=1)
    target = jnp.where(slot_rank < capacity, flat_ids * capacity + slot_rank, -1).reshape(
        tok_rows, top_k
    )
    slot_ids = jnp.arange(experts * capacity, dtype=jnp.int32)
    return (target[:, :, None] == slot_ids[None, None, :]).astype(jnp.float32)


def dispatch_rows(tokens, route, quant, capacity, experts):
    chosen = slot_choice(route, capacity, experts)
    picker = jnp.sum(chosen, axis=1).astype(jnp.bfloat16)
    send_x = jnp.einsum("ts,td->sd", picker, tokens[0], preferred_element_type=jnp.float32).astype(
        jnp.bfloat16
    )
    send_p = (jnp.einsum("tks,tk->s", chosen, quant[0].astype(jnp.float32)) / 256.0).astype(
        jnp.bfloat16
    )
    return (send_x.reshape(experts, capacity, -1), send_p.reshape(experts, capacity))


def per_device(
    x_prev_a,
    route_a,
    prob_a,
    w_gate,
    w_up,
    route_b,
    prob_b,
    saved_gate_b,
    saved_up_b,
    grad_hidden_b,
):
    experts = lax.axis_size("expert")
    capacity = saved_gate_b.shape[3]
    width = x_prev_a.shape[2]
    units = saved_gate_b.shape[4]
    gate_weight = w_gate[0]
    up_weight = w_up[0]
    x_here = passed_along(x_prev_a, "pipe", 1)
    send_x, send_p = dispatch_rows(x_here, route_a, prob_a, capacity, experts)
    recv_x, recv_p = (
        lax.all_to_all(send_x, "expert", split_axis=0, concat_axis=0, tiled=True),
        lax.all_to_all(send_p, "expert", split_axis=0, concat_axis=0, tiled=True),
    )
    rows = recv_x.reshape(-1, width)
    gate = jnp.dot(rows, gate_weight, preferred_element_type=jnp.float32)
    up_proj = jnp.dot(rows, up_weight, preferred_element_type=jnp.float32)
    scale = recv_p.reshape(-1, 1).astype(jnp.float32)
    hidden = (scale * jax.nn.silu(gate) * up_proj).astype(jnp.bfloat16)
    hidden_a = hidden.reshape(1, 1, experts, capacity, units)
    g_val = saved_gate_b[0, 0].reshape(-1, units).astype(jnp.float32)
    u_val = saved_up_b[0, 0].reshape(-1, units).astype(jnp.float32)
    dh_val = grad_hidden_b[0, 0].reshape(-1, units).astype(jnp.float32)
    p_val = prob_b[0, 0].reshape(-1, 1).astype(jnp.float32)
    sigma = jax.nn.sigmoid(g_val)
    active = g_val * sigma
    scaled = dh_val * p_val
    d_up = (scaled * active).astype(jnp.bfloat16)
    d_gate = (scaled * u_val * sigma * (1.0 + g_val * (1.0 - sigma))).astype(jnp.bfloat16)
    slot_dx = (
        jnp.einsum("rh,dh->rd", d_gate, gate_weight, preferred_element_type=jnp.float32)
        + jnp.einsum("rh,dh->rd", d_up, up_weight, preferred_element_type=jnp.float32)
    ).astype(jnp.bfloat16)
    slot_dp = jnp.sum(dh_val * active * u_val, axis=1).astype(jnp.bfloat16)
    back_x, back_p = (
        lax.all_to_all(
            slot_dx.reshape(experts, capacity, width),
            "expert",
            split_axis=0,
            concat_axis=0,
            tiled=True,
        ),
        lax.all_to_all(
            slot_dp.reshape(experts, capacity), "expert", split_axis=0, concat_axis=0, tiled=True
        ),
    )
    chosen_b = slot_choice(route_b, capacity, experts)
    picker_b = jnp.sum(chosen_b, axis=1).astype(jnp.bfloat16)
    grad_tokens = jnp.dot(
        picker_b, back_x.reshape(-1, width), preferred_element_type=jnp.float32
    ).astype(jnp.bfloat16)
    grad_prob = jnp.einsum("tks,s->tk", chosen_b, back_p.reshape(-1).astype(jnp.float32)).astype(
        jnp.bfloat16
    )
    grad_x_b = passed_along(grad_tokens[None], "pipe", -1)
    return (hidden_a, grad_x_b, grad_prob[None])


MESH = pl.DeviceIdType.MESH


def to_column(row):
    size = row.shape[1]
    eye = lax.broadcasted_iota(jnp.int32, (size, size), 0) == lax.broadcasted_iota(
        jnp.int32, (size, size), 1
    )
    return jnp.sum(jnp.where(eye, jnp.broadcast_to(row, (size, size)), 0.0), axis=1, keepdims=True)


def to_row(column):
    size = column.shape[0]
    eye = lax.broadcasted_iota(jnp.int32, (size, size), 0) == lax.broadcasted_iota(
        jnp.int32, (size, size), 1
    )
    return jnp.sum(
        jnp.where(eye, jnp.broadcast_to(column, (size, size)), 0.0), axis=0, keepdims=True
    )


VMEM_BYTES = 62 * 1024 * 1024 + 512 * 1024
LANES = 128
ROWS_Y = 2
PARTS = 3


SHARES = ((6, True), (6, True), (2, False), (2, False))


def pieces_of(width):
    units, whole = width // LANES, sum(share for share, _ in SHARES)
    pieces, start, taken = [], 0, 0
    for share, z_first in SHARES:
        taken += share
        end = units * taken // whole
        pieces.append((start * LANES, (end - start) * LANES, z_first))
        start = end
    return pieces


COMPUTE = ((0, 0), (0, 1), (0, 2), (0, 3), (1, 0), (1, 1), (1, 2), (1, 3), (2, 0), (2, 1))
ORDERS = (
    (
        (),
        (),
        (),
        (),
        (),
        ((1, 0, 3),),
        ((1, 1, 3),),
        ((1, 1, 2), (2, 2, 3), (1, 0, 2)),
        ((2, 3, 3), (1, 1, 0), (2, 2, 2), (1, 0, 0), (1, 1, 1), (1, 0, 1), (2, 3, 2), (2, 2, 1), (2, 3, 1), (0, 0, 0, 0), (0, 1, 0, 0), (0, 3, 0, 0), (0, 0, 1, 0), (0, 2, 0, 0), (0, 1, 1, 0), (0, 0, 0, 1), (0, 3, 1, 0), (0, 2, 1, 0), (0, 1, 0, 1), (2, 0, 3), (0, 3, 0, 1), (0, 2, 0, 1), (2, 1, 3), (2, 1, 2), (2, 0, 2), (0, 0, 0, 2), (0, 3, 1, 1), (0, 1, 0, 2), (0, 2, 1, 1), (0, 3, 0, 2), (0, 2, 0, 2), (4, 1), (2, 1, 1), (4, 0), (2, 0, 1), (0, 0, 0, 3), (0, 1, 0, 3), (0, 3, 0, 3), (0, 2, 0, 3), (0, 0, 1, 1), (0, 3, 1, 2), (0, 2, 1, 2), (0, 1, 1, 1)),
        ((4, 3), (0, 0, 1, 2), (4, 2), (0, 1, 1, 2), (0, 3, 1, 3), (0, 0, 1, 3), (0, 2, 1, 3), (0, 1, 1, 3)),
        (),
    ),
    (
        (),
        (),
        (),
        (),
        (),
        ((1, 0, 3),),
        ((1, 1, 3), (1, 0, 0), (1, 1, 0)),
        ((1, 1, 1), (1, 1, 2), (1, 0, 1), (1, 0, 2)),
        ((0, 0, 0, 1), (0, 0, 0, 0), (0, 1, 0, 1), (0, 0, 1, 1), (0, 3, 0, 1), (0, 1, 0, 0), (0, 2, 0, 1), (0, 3, 0, 0), (0, 0, 0, 2), (0, 1, 1, 1), (0, 2, 0, 0), (0, 3, 1, 1), (0, 1, 0, 2), (0, 2, 1, 1), (2, 2, 3), (0, 3, 0, 2), (0, 2, 0, 2), (2, 3, 3), (2, 2, 2), (2, 3, 2), (0, 0, 0, 3), (0, 1, 0, 3), (0, 3, 0, 3), (0, 2, 0, 3), (0, 3, 1, 2), (0, 3, 1, 0), (0, 2, 1, 2), (0, 2, 1, 0), (2, 0, 3), (3, 3, 0), (4, 1), (2, 1, 3), (3, 2, 0), (4, 3), (4, 0), (2, 1, 2), (4, 2), (2, 0, 2), (0, 3, 1, 3), (0, 2, 1, 3), (0, 0, 1, 0), (3, 0, 0), (0, 1, 1, 0)),
        ((3, 1, 0), (0, 0, 1, 2), (0, 1, 1, 2), (0, 0, 1, 3), (0, 1, 1, 3)),
        (),
    ),
    (
        (),
        (),
        (),
        (),
        (),
        ((1, 0, 0),),
        ((1, 1, 0),),
        (),
        ((1, 1, 1), (1, 0, 1), (1, 1, 2), (1, 0, 2), (1, 1, 3), (1, 0, 3), (0, 0, 0, 2), (0, 1, 0, 2), (0, 0, 0, 1), (0, 0, 0, 3), (0, 0, 1, 2), (0, 3, 0, 2), (0, 2, 0, 2), (0, 1, 0, 3), (0, 1, 0, 1), (0, 1, 1, 2), (0, 3, 0, 3), (0, 2, 0, 3), (0, 3, 0, 1), (0, 3, 1, 2), (0, 2, 0, 1), (0, 2, 1, 2), (3, 3, 0), (0, 0, 0, 0), (3, 2, 0), (3, 3, 1), (0, 1, 0, 0), (0, 3, 0, 0), (0, 2, 0, 0), (3, 2, 1), (0, 3, 1, 1), (2, 2, 3), (0, 2, 1, 1), (0, 3, 1, 3), (0, 2, 1, 3), (2, 3, 3), (4, 2), (3, 0, 0), (4, 1), (4, 3), (4, 0), (3, 1, 0), (0, 3, 1, 0), (0, 2, 1, 0), (3, 1, 1), (2, 0, 3), (3, 0, 1), (0, 0, 1, 1), (0, 0, 1, 3), (2, 1, 3), (0, 1, 1, 1), (0, 1, 1, 3)),
        ((0, 0, 1, 0), (0, 1, 1, 0)),
        (),
    ),
    (
        (),
        (),
        (),
        (),
        (),
        ((1, 0, 0),),
        ((1, 1, 0),),
        (),
        ((1, 1, 1), (1, 0, 1), (3, 3, 0), (3, 2, 0), (3, 3, 1), (1, 1, 2), (1, 0, 2), (3, 2, 1), (1, 1, 3), (3, 3, 2), (1, 0, 3), (3, 2, 2), (0, 0, 0, 3), (0, 1, 0, 3), (0, 0, 1, 3), (0, 0, 0, 2), (0, 3, 0, 3), (0, 1, 1, 3), (0, 2, 0, 3), (0, 3, 1, 3), (0, 1, 0, 2), (0, 2, 1, 3), (0, 3, 0, 2), (0, 2, 0, 2), (3, 0, 0), (3, 1, 0), (0, 0, 0, 1), (0, 1, 0, 1), (3, 1, 1), (0, 3, 0, 1), (3, 0, 1), (0, 3, 1, 2), (0, 2, 0, 1), (0, 2, 1, 2), (3, 1, 2), (3, 0, 2), (0, 0, 0, 0), (4, 1), (0, 1, 0, 0), (0, 3, 0, 0), (4, 0), (0, 2, 0, 0), (0, 3, 1, 1), (4, 2), (0, 2, 1, 1), (0, 0, 1, 2), (0, 1, 1, 2)),
        ((4, 3), (0, 3, 1, 0), (0, 0, 1, 1), (0, 2, 1, 0), (0, 1, 1, 1), (0, 0, 1, 0), (0, 1, 1, 0)),
        (),
    ),
)


def mesh_kernel(
    n,
    sections,
    x_hbm,
    route_a_hbm,
    prob_a_hbm,
    route_b_hbm,
    prob_b_hbm,
    wg_hbm,
    wu_hbm,
    g_hbm,
    u_hbm,
    dh_hbm,
    hidden_ref,
    gx_ref,
    gp_ref,
    route_a_ref,
    prob_a_ref,
    route_b_ref,
    prob_b_ref,
    wg,
    wu,
    g_buf,
    u_buf,
    dh_buf,
    d_gate,
    d_up,
    rows,
    dx,
    in_up,
    in_down,
    in_y,
    fin_in,
    tabs,
    dps,
    dps_up,
    dps_down,
    dps_over,
    load_sem,
    weight_sem,
    shift_send,
    tab_send,
    tab_recv,
    dps_send,
    dps_recv,
    ag_send,
    ag_recv,
    up_send,
    up_recv,
    down_send,
    down_recv,
    y_send,
    y_recv,
    fin_send,
    fin_recv,
):
    tok, width = x_hbm.shape
    units = wg.shape[1]
    pieces = pieces_of(width)
    nz = n // ROWS_Y
    sec = lax.axis_index("pipe")
    me = lax.axis_index("expert")
    z, y = lax.div(me, ROWS_Y), lax.rem(me, ROWS_Y)
    after = lax.rem(sec + 1, sections)
    before = lax.rem(sec + sections - 1, sections)
    across = me + 1 - 2 * y
    top = nz - 1

    loads = [
        pltpu.make_async_copy(src, dst, load_sem.at[i])
        for i, (src, dst) in enumerate(
            (
                (route_a_hbm, route_a_ref),
                (prob_a_hbm, prob_a_ref),
                (route_b_hbm, route_b_ref),
                (prob_b_hbm, prob_b_ref),
                (g_hbm, g_buf),
                (u_hbm, u_buf),
                (dh_hbm, dh_buf),
            )
        )
    ]
    for load in loads:
        load.start()

    barrier = pltpu.get_barrier_semaphore()

    def greet(peer):
        pl.semaphore_signal(barrier, inc=1, device_id=peer, device_id_type=MESH)

    for peer in ((after, me), (before, me)):
        greet(peer)
    for section in (sec, after, before):
        greet((section, across))

        @pl.when(z < top)
        def _():
            greet((section, me + ROWS_Y))

        @pl.when(z > 0)
        def _():
            greet((section, me - ROWS_Y))

    weights = {}
    for c in [c for what, c in COMPUTE if what == 1]:
        start, size, _ = pieces[c]
        span = pl.ds(start, size)
        weights[c] = [
            pltpu.make_async_copy(src.at[span, :], dst.at[span, :], weight_sem.at[i, c])
            for i, (src, dst) in enumerate(((wg_hbm, wg), (wu_hbm, wu)))
        ]
        for load in weights[c]:
            load.start()

    def cols(c):
        start, size, _ = pieces[c]
        return pl.ds(start, size)

    last = len(pieces) - 1
    for load in loads[:2]:
        load.wait()
    route_a = route_a_ref[...]
    prob_a = prob_a_ref[...]
    by_expert = jnp.concatenate(
        [jnp.sum(jnp.where(route_a == e, prob_a, 0), axis=0, keepdims=True) for e in range(n)],
        axis=0,
    )
    tabs[me] = jnp.zeros(tabs.shape[1:], tabs.dtype)
    tabs[me, 0:n, 0:tok] = by_expert.astype(jnp.float32).astype(jnp.bfloat16)

    pl.semaphore_wait(
        barrier,
        5 + 3 * jnp.where(z < top, 1, 0) + 3 * jnp.where(z > 0, 1, 0),
    )

    for c in range(len(pieces)):
        if pieces[c][2]:

            @pl.when(z == 0)
            def _():
                fin_in[1, :, cols(c)] = jnp.zeros((tok, pieces[c][1]), fin_in.dtype)

            @pl.when(z == top)
            def _():
                fin_in[2, :, cols(c)] = jnp.zeros((tok, pieces[c][1]), fin_in.dtype)

    started = []

    def remote(src, dst, send_sem, recv_sem, device):
        return pltpu.make_async_remote_copy(
            src_ref=src,
            dst_ref=dst,
            send_sem=send_sem,
            recv_sem=recv_sem,
            device_id=device,
            device_id_type=MESH,
        )

    def arrived(dst, recv_sem):
        remote(dst, dst, recv_sem, recv_sem, (sec, across)).wait_recv()

    def at(zz):
        return pl.when(z == zz)

    UP, DOWN, OVER = 0, 1, 2

    def toward(way):
        return (sec, (me + ROWS_Y, me - ROWS_Y, across)[way])

    def post(zz, copy):
        remote(*copy()).start()
        started.append((zz, copy))

    def neighbours():
        yield None, OVER, across, 1
        for zz in range(nz):
            if zz < top:
                yield zz, UP, me + ROWS_Y, 0
            if zz > 0:
                yield zz, DOWN, me - ROWS_Y, 0

    def first(zz, way, there, v, c):
        def copy():
            if c is None:
                held = tabs.at[me]
                return held, held, tab_send.at[0, z, way], tab_recv.at[v, z], (sec, there)
            span = cols(c)
            held = rows.at[me, :, span]
            return x_hbm.at[:, span], held, shift_send.at[c, way], ag_recv.at[c, v, z], (after, there)

        post(zz, copy)

    for c in [*range(len(pieces)), None]:
        for zz, way, there, v in neighbours():
            if zz is None:
                first(zz, way, there, v, c)
            else:

                @at(zz)
                def _():
                    first(zz, way, there, v, c)

        if c is not None:
            post(
                None,
                lambda c=c: (
                    x_hbm.at[:, cols(c)],
                    rows.at[me, :, cols(c)],
                    shift_send.at[c, 3],
                    ag_recv.at[c, 0, z],
                    (after, me),
                ),
            )

    def expert_at(zz, v):
        return ROWS_Y * zz + (y if v == 0 else 1 - y)

    def ways_of(zz, c, v, zs):
        z_first = pieces[c][2]
        ways = []
        if v == 0 and zs == zz:
            return ways
        if zs <= zz and zz < top and not (z_first and v == 1):
            ways.append(UP)
        if zs >= zz and zz > 0 and not (z_first and v == 1):
            ways.append(DOWN)
        if v == 0 and z_first:
            ways.append(OVER)
        return ways

    def spread_block(zz, c, v, zs):
        block = expert_at(zs, v)
        arrived(rows.at[block, :, cols(c)], ag_recv.at[c, v, zs])
        with_table = c == last and not (v == 0 and zs == zz)
        if with_table:
            arrived(tabs.at[block], tab_recv.at[v, zs])
        for way in ways_of(zz, c, v, zs):

            def copy(way=way):
                held = rows.at[expert_at(zs, v), :, cols(c)]
                there = 1 if way == OVER else v
                recv = ag_recv.at[c, there, zs]
                return held, held, ag_send.at[c, v, zs, way], recv, toward(way)

            post(zz, copy)
            if with_table:

                def small(way=way):
                    held = tabs.at[expert_at(zs, v)]
                    recv = tab_recv.at[1 if way == OVER else v, zs]
                    return held, held, tab_send.at[v, zs, way], recv, toward(way)

                post(zz, small)

    def backward_rows(j):
        span = pl.ds(j * tok, tok)
        g_val = g_buf[span, :].astype(jnp.float32)
        u_val = u_buf[span, :].astype(jnp.float32)
        dh_val = dh_buf[span, :].astype(jnp.float32)
        p_val = to_column(prob_b_ref[pl.ds(j, 1), :].astype(jnp.float32))
        sigma = jax.nn.sigmoid(g_val)
        active = g_val * sigma
        scaled = dh_val * p_val
        d_up[span, :] = (scaled * active).astype(jnp.bfloat16)
        d_gate[span, :] = (scaled * u_val * sigma * (1.0 + g_val * (1.0 - sigma))).astype(
            jnp.bfloat16
        )
        column = jnp.sum(dh_val * active * u_val, axis=1, keepdims=True)
        row = to_row(column)
        line = lax.broadcasted_iota(jnp.int32, (dps.shape[1], tok), 0)
        dps[j] = jnp.zeros(dps.shape[1:], dps.dtype)
        dps[j, :, 0:tok] = jnp.where(line == me, row, 0.0).astype(jnp.bfloat16)

    contract = (((1,), (1,)), ((), ()))

    def gradient(c):
        for load in weights[c]:
            load.wait()
        span = cols(c)
        out = lax.dot_general(
            d_gate[...], wg[span, :], contract, preferred_element_type=jnp.float32
        ) + lax.dot_general(d_up[...], wu[span, :], contract, preferred_element_type=jnp.float32)
        dx[:, :, span] = out.reshape(n, tok, out.shape[1]).astype(jnp.bfloat16)

    def f32(ref_value):
        return ref_value.astype(jnp.float32)

    def trade(zz, c, zt):
        post(
            zz,
            lambda: (
                dx.at[expert_at(zt, 1), :, cols(c)],
                in_y.at[zt, :, cols(c)],
                y_send.at[c, zt],
                y_recv.at[c, zt],
                toward(OVER),
            ),
        )

    def pass_on(zz, c, zt, way):
        z_first = pieces[c][2]
        inbox = in_up if way == UP else in_down
        send_sem, recv_sem = (up_send, up_recv) if way == UP else (down_send, down_recv)
        begins = zz == 0 if way == UP else zz == top
        if z_first:
            here = expert_at(zt, 0)
            total = f32(dx[here, :, cols(c)])
            arrived(in_y.at[zt, :, cols(c)], y_recv.at[c, zt])
            total = total + f32(in_y[zt, :, cols(c)])
            if not begins:
                arrived(inbox.at[here, :, cols(c)], recv_sem.at[c, zt])
                total = total + f32(inbox[here, :, cols(c)])
            dx[here, :, cols(c)] = total.astype(jnp.bfloat16)
        else:
            pair = pl.ds(ROWS_Y * zt, ROWS_Y)
            if not begins:
                arrived(inbox.at[pair, :, cols(c)], recv_sem.at[c, zt])
                total = f32(dx[pair, :, cols(c)]) + f32(inbox[pair, :, cols(c)])
                dx[pair, :, cols(c)] = total.astype(jnp.bfloat16)
                if c == last:
                    small_in = dps_up if way == UP else dps_down
                    arrived(small_in.at[pair], dps_recv.at[way, zt])
                    dps[pair] = (f32(dps[pair]) + f32(small_in[pair])).astype(jnp.bfloat16)
        def copy():
            block = expert_at(zt, 0) if z_first else pl.ds(ROWS_Y * zt, ROWS_Y)
            src, dst = dx.at[block, :, cols(c)], inbox.at[block, :, cols(c)]
            if z_first and abs(zt - zz) == 1:
                there = (before, toward(way)[1])
                return src, fin_in.at[1 + way, :, cols(c)], fin_send.at[c, 1 + way], fin_recv.at[c, 1 + way], there
            return src, dst, send_sem.at[c, zt], recv_sem.at[c, zt], toward(way)

        post(zz, copy)
        if c == last:

            def small():
                pair = pl.ds(ROWS_Y * zt, ROWS_Y)
                dst = (dps_up if way == UP else dps_down).at[pair]
                return dps.at[pair], dst, dps_send.at[way, zt], dps_recv.at[way, zt], toward(way)

            post(zz, small)

    def line_total(zz, c, block):
        total = f32(dx[block, :, cols(c)])
        if zz > 0:
            total = total + f32(in_up[block, :, cols(c)])
        if zz < top:
            total = total + f32(in_down[block, :, cols(c)])
        return total

    def own_line(zz, c):
        z_first = pieces[c][2]
        own, other = expert_at(zz, 0), expert_at(zz, 1)
        if z_first:
            arrived(in_y.at[zz, :, cols(c)], y_recv.at[c, zz])
            total = f32(dx[own, :, cols(c)]) + f32(in_y[zz, :, cols(c)])
            dx[own, :, cols(c)] = total.astype(jnp.bfloat16)
        else:
            pair = pl.ds(ROWS_Y * zz, ROWS_Y)
            if zz > 0:
                arrived(in_up.at[pair, :, cols(c)], up_recv.at[c, zz])
            if zz < top:
                arrived(in_down.at[pair, :, cols(c)], down_recv.at[c, zz])
            dx[other, :, cols(c)] = line_total(zz, c, other).astype(jnp.bfloat16)
            post(
                zz,
                lambda: (
                    dx.at[expert_at(zz, 1), :, cols(c)],
                    fin_in.at[1, :, cols(c)],
                    fin_send.at[c, 1],
                    fin_recv.at[c, 1],
                    (before, across),
                ),
            )
            if c == last:
                small = f32(dps[pair])
                if zz > 0:
                    arrived(dps_up.at[pair], dps_recv.at[UP, zz])
                    small = small + f32(dps_up[pair])
                if zz < top:
                    arrived(dps_down.at[pair], dps_recv.at[DOWN, zz])
                    small = small + f32(dps_down[pair])
                dps[pair] = small.astype(jnp.bfloat16)
                post(
                    zz,
                    lambda: (
                        dps.at[expert_at(zz, 1)],
                        dps_over,
                        dps_send.at[OVER, zz],
                        dps_recv.at[OVER, zz],
                        toward(OVER),
                    ),
                )
            dx[own, :, cols(c)] = line_total(zz, c, own).astype(jnp.bfloat16)
        post(
            zz,
            lambda: (
                dx.at[expert_at(zz, 0), :, cols(c)],
                fin_in.at[0, :, cols(c)],
                fin_send.at[c, 0],
                fin_recv.at[c, 0],
                (before, me),
            ),
        )

    group = n // 2
    near = lax.div(z, nz // 2)

    def hidden_part(half, k):
        part = units // PARTS
        span = pl.ds(k * part, part)
        blocks = pl.ds(half * group, group)
        tokens = rows[blocks, :, pl.ds(0, width)].reshape(group * tok, width)
        gate = jnp.dot(tokens, wg[:, span], preferred_element_type=jnp.float32)
        up = jnp.dot(tokens, wu[:, span], preferred_element_type=jnp.float32)
        table = tabs[blocks, 0:n, 0:tok].astype(jnp.float32)
        mine = lax.broadcasted_iota(jnp.int32, table.shape, 1) == me
        table = jnp.sum(jnp.where(mine, table, 0.0), axis=1) / 256.0
        scale = jnp.concatenate([to_column(table[j : j + 1, :]) for j in range(group)], axis=0)
        lines = pl.ds(pl.multiple_of(half * (group * tok), group * tok), group * tok)
        hidden_ref[lines, span] = (scale * jax.nn.silu(gate) * up).astype(jnp.bfloat16)

    def load_saved():
        for load in loads[3:]:
            load.wait()

    def pick():
        loads[2].wait()
        arrived(dps_over, dps_recv.at[OVER, z])
        by_slot = f32(dps[me]) + f32(dps_over[...])
        route_b = route_b_ref[...]
        picked = jnp.zeros(route_b.shape, jnp.float32)
        for e in range(n):
            picked = picked + jnp.where(route_b == e, by_slot[e : e + 1, 0:tok], 0.0)
        gp_ref[...] = picked.astype(jnp.bfloat16)

    def step(zz, what, c, *rest):
        if what == 0:
            spread_block(zz, c, *rest)
        elif what == 1:
            trade(zz, c, *rest)
        elif what == 4:
            own_line(zz, c)
        else:
            pass_on(zz, c, *rest, UP if what == 2 else DOWN)

    def work(what, k):
        share = n // sum(1 for kind, _ in COMPUTE if kind == 0)
        if what == 0:
            if k == 0:
                load_saved()
            for j in range(k * share, (k + 1) * share):
                backward_rows(j)
        elif what == 1:
            gradient(k)
        else:
            for part in range(PARTS):
                hidden_part(near if k == 0 else 1 - near, part)

    for i in range(len(COMPUTE) + 1):
        for zz in range(nz):
            if ORDERS[zz][i]:

                @at(zz)
                def _():
                    for each in ORDERS[zz][i]:
                        step(zz, *each)

        if i < len(COMPUTE):
            work(*COMPUTE[i])

    pick()
    for c in range(len(pieces)):
        span = cols(c)
        arrived(fin_in.at[0, :, span], fin_recv.at[c, 0])
        if pieces[c][2]:

            @pl.when(z > 0)
            def _():
                arrived(fin_in.at[1, :, span], fin_recv.at[c, 1])

            @pl.when(z < top)
            def _():
                arrived(fin_in.at[2, :, span], fin_recv.at[c, 2])

            total = f32(fin_in[0, :, span]) + f32(fin_in[1, :, span]) + f32(fin_in[2, :, span])
        else:
            arrived(fin_in.at[1, :, span], fin_recv.at[c, 1])
            total = f32(fin_in[0, :, span]) + f32(fin_in[1, :, span])
        gx_ref[:, span] = total.astype(jnp.bfloat16)
    for zz in [None, *range(nz)]:
        copies = [copy for where, copy in started if where == zz]
        if zz is None:
            for copy in copies:
                remote(*copy()).wait_send()
        else:

            @at(zz)
            def _():
                for copy in copies:
                    remote(*copy()).wait_send()


def put_kernel(a_ref, b_ref, c_ref, a_out, b_out, c_out, sem):
    held = ((a_ref, a_out), (b_ref, b_out), (c_ref, c_out))
    puts = [pltpu.make_async_copy(src, dst, sem.at[i]) for i, (src, dst) in enumerate(held)]
    for put in puts:
        put.start()
    for put in puts:
        put.wait()


def full_routing(
    x_prev_a,
    route_a,
    prob_a,
    w_gate,
    w_up,
    route_b,
    prob_b,
    saved_gate_b,
    saved_up_b,
    grad_hidden_b,
):
    n = lax.axis_size("expert")
    sections = lax.axis_size("pipe")
    tok, width = x_prev_a.shape[1:]
    top_k = route_a.shape[2]
    units = saved_gate_b.shape[4]
    slots = n * tok
    nz = n // ROWS_Y
    count = len(pieces_of(width))
    small = (16 * pl.cdiv(n, 16), LANES * pl.cdiv(tok, LANES))
    bf16 = jnp.bfloat16
    dma = pltpu.SemaphoreType.DMA
    any_ = pl.BlockSpec(memory_space=pl.ANY)
    vmem = pl.BlockSpec(memory_space=pltpu.VMEM)
    hidden, grad_x, grad_prob = pl.pallas_call(
        functools.partial(mesh_kernel, n, sections),
        out_shape=(
            pltpu.VMEM((slots, units), bf16),
            pltpu.VMEM((tok, width), bf16),
            pltpu.VMEM((top_k, tok), bf16),
        ),
        in_specs=[any_] * 10,
        out_specs=(vmem,) * 3,
        scratch_shapes=[
            pltpu.VMEM((top_k, tok), jnp.int32),
            pltpu.VMEM((top_k, tok), jnp.int32),
            pltpu.VMEM((top_k, tok), jnp.int32),
            pltpu.VMEM((n, tok), bf16),
            pltpu.VMEM((width, units), bf16),
            pltpu.VMEM((width, units), bf16),
            pltpu.VMEM((slots, units), bf16),
            pltpu.VMEM((slots, units), bf16),
            pltpu.VMEM((slots, units), bf16),
            pltpu.VMEM((slots, units), bf16),
            pltpu.VMEM((slots, units), bf16),
            pltpu.VMEM((n, tok, width), bf16),
            pltpu.VMEM((n, tok, width), bf16),
            pltpu.VMEM((n, tok, width), bf16),
            pltpu.VMEM((n, tok, width), bf16),
            pltpu.VMEM((nz, tok, width), bf16),
            pltpu.VMEM((3, tok, width), bf16),
            pltpu.VMEM((n, *small), bf16),
            pltpu.VMEM((n, *small), bf16),
            pltpu.VMEM((n, *small), bf16),
            pltpu.VMEM((n, *small), bf16),
            pltpu.VMEM(small, bf16),
            dma((7,)),
            dma((2, count)),
            dma((count, 4)),
            dma((2, nz, 3)),
            dma((2, nz)),
            dma((3, nz)),
            dma((3, nz)),
            dma((count, 2, nz, 3)),
            dma((count, 2, nz)),
            dma((count, nz)),
            dma((count, nz)),
            dma((count, nz)),
            dma((count, nz)),
            dma((count, nz)),
            dma((count, nz)),
            dma((count, 3)),
            dma((count, 3)),
        ],
        compiler_params=pltpu.CompilerParams(
            collective_id=0, has_side_effects=True, vmem_limit_bytes=VMEM_BYTES
        ),
        name="mesh",
    )(
        x_prev_a[0],
        route_a[0].T,
        prob_a[0].T,
        route_b[0].T,
        prob_b[0, 0],
        w_gate[0],
        w_up[0],
        saved_gate_b.reshape(slots, units),
        saved_up_b.reshape(slots, units),
        grad_hidden_b.reshape(slots, units),
    )
    results = (hidden, grad_x, grad_prob)
    hidden, grad_x, grad_prob = pl.pallas_call(
        put_kernel,
        out_shape=tuple(jax.ShapeDtypeStruct(a.shape, a.dtype) for a in results),
        in_specs=[any_] * 3,
        out_specs=(any_,) * 3,
        scratch_shapes=[dma((3,))],
        compiler_params=pltpu.CompilerParams(vmem_limit_bytes=1 << 20),
        name="put",
    )(*results)
    return (
        hidden.reshape(1, 1, n, tok, units),
        grad_x[None],
        grad_prob.T[None],
    )


def any_routing(*args):
    tokens, top_k = args[1].shape[1:]
    capacity = args[7].shape[3]
    full = top_k == lax.axis_size("expert") and capacity == tokens
    if full and top_k == 8 == ROWS_Y * len(ORDERS) and lax.axis_size("pipe") > 2:
        return full_routing(*args)
    return per_device(*args)


def solution(mesh):
    return jax.shard_map(
        any_routing,
        mesh=mesh,
        in_specs=(
            P("pipe", "expert", None),
            P("pipe", "expert", None),
            P("pipe", "expert", None),
            P("expert", None, None),
            P("expert", None, None),
            P("pipe", "expert", None),
            P("pipe", "expert", None, None),
            P("pipe", "expert", None, None, None),
            P("pipe", "expert", None, None, None),
            P("pipe", "expert", None, None, None),
        ),
        out_specs=(
            P("pipe", "expert", None, None, None),
            P("pipe", "expert", None),
            P("pipe", "expert", None),
        ),
        check_vma=False,
    )
```

```python
import functools

import jax
import jax.numpy as jnp
from jax import lax
from jax.experimental import pallas as pl
from jax.experimental.pallas import tpu as pltpu
from jax.sharding import PartitionSpec as P


def passed_along(block, axis, distance):
    devices = range(lax.axis_size(axis))
    route = [((i - distance) % len(devices), i) for i in devices]
    return lax.ppermute(block, axis, route)


def slot_choice(route, capacity, experts):
    expert_ids = route[0]
    tok_rows, top_k = expert_ids.shape
    flat_ids = expert_ids.reshape(-1)
    onehot = (flat_ids[:, None] == jnp.arange(experts, dtype=jnp.int32)[None, :]).astype(jnp.int32)
    rows = flat_ids.shape[0]
    earlier = jnp.arange(rows)[:, None] > jnp.arange(rows)[None, :]
    before = jnp.dot(
        earlier.astype(jnp.bfloat16),
        onehot.astype(jnp.bfloat16),
        preferred_element_type=jnp.float32,
    ).astype(jnp.int32)
    slot_rank = jnp.sum(before * onehot, axis=1)
    target = jnp.where(slot_rank < capacity, flat_ids * capacity + slot_rank, -1).reshape(
        tok_rows, top_k
    )
    slot_ids = jnp.arange(experts * capacity, dtype=jnp.int32)
    return (target[:, :, None] == slot_ids[None, None, :]).astype(jnp.float32)


def dispatch_rows(tokens, route, quant, capacity, experts):
    chosen = slot_choice(route, capacity, experts)
    picker = jnp.sum(chosen, axis=1).astype(jnp.bfloat16)
    send_x = jnp.einsum("ts,td->sd", picker, tokens[0], preferred_element_type=jnp.float32).astype(
        jnp.bfloat16
    )
    send_p = (jnp.einsum("tks,tk->s", chosen, quant[0].astype(jnp.float32)) / 256.0).astype(
        jnp.bfloat16
    )
    return (send_x.reshape(experts, capacity, -1), send_p.reshape(experts, capacity))


def per_device(
    x_prev_a,
    route_a,
    prob_a,
    w_gate,
    w_up,
    route_b,
    prob_b,
    saved_gate_b,
    saved_up_b,
    grad_hidden_b,
):
    experts = lax.axis_size("expert")
    capacity = saved_gate_b.shape[3]
    width = x_prev_a.shape[2]
    units = saved_gate_b.shape[4]
    gate_weight = w_gate[0]
    up_weight = w_up[0]
    x_here = passed_along(x_prev_a, "pipe", 1)
    send_x, send_p = dispatch_rows(x_here, route_a, prob_a, capacity, experts)
    recv_x, recv_p = (
        lax.all_to_all(send_x, "expert", split_axis=0, concat_axis=0, tiled=True),
        lax.all_to_all(send_p, "expert", split_axis=0, concat_axis=0, tiled=True),
    )
    rows = recv_x.reshape(-1, width)
    gate = jnp.dot(rows, gate_weight, preferred_element_type=jnp.float32)
    up_proj = jnp.dot(rows, up_weight, preferred_element_type=jnp.float32)
    scale = recv_p.reshape(-1, 1).astype(jnp.float32)
    hidden = (scale * jax.nn.silu(gate) * up_proj).astype(jnp.bfloat16)
    hidden_a = hidden.reshape(1, 1, experts, capacity, units)
    g_val = saved_gate_b[0, 0].reshape(-1, units).astype(jnp.float32)
    u_val = saved_up_b[0, 0].reshape(-1, units).astype(jnp.float32)
    dh_val = grad_hidden_b[0, 0].reshape(-1, units).astype(jnp.float32)
    p_val = prob_b[0, 0].reshape(-1, 1).astype(jnp.float32)
    sigma = jax.nn.sigmoid(g_val)
    active = g_val * sigma
    scaled = dh_val * p_val
    d_up = (scaled * active).astype(jnp.bfloat16)
    d_gate = (scaled * u_val * sigma * (1.0 + g_val * (1.0 - sigma))).astype(jnp.bfloat16)
    slot_dx = (
        jnp.einsum("rh,dh->rd", d_gate, gate_weight, preferred_element_type=jnp.float32)
        + jnp.einsum("rh,dh->rd", d_up, up_weight, preferred_element_type=jnp.float32)
    ).astype(jnp.bfloat16)
    slot_dp = jnp.sum(dh_val * active * u_val, axis=1).astype(jnp.bfloat16)
    back_x, back_p = (
        lax.all_to_all(
            slot_dx.reshape(experts, capacity, width),
            "expert",
            split_axis=0,
            concat_axis=0,
            tiled=True,
        ),
        lax.all_to_all(
            slot_dp.reshape(experts, capacity), "expert", split_axis=0, concat_axis=0, tiled=True
        ),
    )
    chosen_b = slot_choice(route_b, capacity, experts)
    picker_b = jnp.sum(chosen_b, axis=1).astype(jnp.bfloat16)
    grad_tokens = jnp.dot(
        picker_b, back_x.reshape(-1, width), preferred_element_type=jnp.float32
    ).astype(jnp.bfloat16)
    grad_prob = jnp.einsum("tks,s->tk", chosen_b, back_p.reshape(-1).astype(jnp.float32)).astype(
        jnp.bfloat16
    )
    grad_x_b = passed_along(grad_tokens[None], "pipe", -1)
    return (hidden_a, grad_x_b, grad_prob[None])


MESH = pl.DeviceIdType.MESH


def to_column(row):
    size = row.shape[1]
    eye = lax.broadcasted_iota(jnp.int32, (size, size), 0) == lax.broadcasted_iota(
        jnp.int32, (size, size), 1
    )
    return jnp.sum(jnp.where(eye, jnp.broadcast_to(row, (size, size)), 0.0), axis=1, keepdims=True)


def to_row(column):
    size = column.shape[0]
    eye = lax.broadcasted_iota(jnp.int32, (size, size), 0) == lax.broadcasted_iota(
        jnp.int32, (size, size), 1
    )
    return jnp.sum(
        jnp.where(eye, jnp.broadcast_to(column, (size, size)), 0.0), axis=0, keepdims=True
    )


VMEM_BYTES = 62 * 1024 * 1024 + 512 * 1024
LANES = 128
ROWS_Y = 2
PARTS = 3


SHARES = ((6, True), (6, True), (2, False), (2, False))


def pieces_of(width):
    units, whole = width // LANES, sum(share for share, _ in SHARES)
    pieces, start, taken = [], 0, 0
    for share, z_first in SHARES:
        taken += share
        end = units * taken // whole
        pieces.append((start * LANES, (end - start) * LANES, z_first))
        start = end
    return pieces


COMPUTE = ((0, 0), (0, 1), (0, 2), (0, 3), (1, 0), (1, 1), (1, 2), (1, 3), (2, 0), (2, 1))
ORDERS = (
    (
        (),
        (),
        (),
        (),
        (),
        ((1, 0, 3),),
        ((1, 1, 3),),
        ((1, 1, 2), (2, 2, 3), (1, 0, 2)),
        ((2, 3, 3), (1, 1, 0), (2, 2, 2), (1, 0, 0), (1, 1, 1), (1, 0, 1), (2, 3, 2), (2, 2, 1), (2, 3, 1), (0, 0, 0, 0), (0, 1, 0, 0), (0, 3, 0, 0), (0, 0, 1, 0), (0, 2, 0, 0), (0, 1, 1, 0), (0, 0, 0, 1), (0, 3, 1, 0), (0, 2, 1, 0), (0, 1, 0, 1), (2, 0, 3), (0, 3, 0, 1), (0, 2, 0, 1), (2, 1, 3), (2, 1, 2), (2, 0, 2), (0, 0, 0, 2), (0, 3, 1, 1), (0, 1, 0, 2), (0, 2, 1, 1), (0, 3, 0, 2), (0, 2, 0, 2), (4, 1), (2, 1, 1), (4, 0), (2, 0, 1), (0, 0, 0, 3), (0, 1, 0, 3), (0, 3, 0, 3), (0, 2, 0, 3), (0, 0, 1, 1), (0, 3, 1, 2), (0, 2, 1, 2), (0, 1, 1, 1)),
        ((4, 3), (0, 0, 1, 2), (4, 2), (0, 1, 1, 2), (0, 3, 1, 3), (0, 0, 1, 3), (0, 2, 1, 3), (0, 1, 1, 3)),
        (),
    ),
    (
        (),
        (),
        (),
        (),
        (),
        ((1, 0, 3),),
        ((1, 1, 3), (1, 0, 0), (1, 1, 0)),
        ((1, 1, 1), (1, 1, 2), (1, 0, 1), (1, 0, 2)),
        ((0, 0, 0, 1), (0, 0, 0, 0), (0, 1, 0, 1), (0, 0, 1, 1), (0, 3, 0, 1), (0, 1, 0, 0), (0, 2, 0, 1), (0, 3, 0, 0), (0, 0, 0, 2), (0, 1, 1, 1), (0, 2, 0, 0), (0, 3, 1, 1), (0, 1, 0, 2), (0, 2, 1, 1), (2, 2, 3), (0, 3, 0, 2), (0, 2, 0, 2), (2, 3, 3), (2, 2, 2), (2, 3, 2), (0, 0, 0, 3), (0, 1, 0, 3), (0, 3, 0, 3), (0, 2, 0, 3), (0, 3, 1, 2), (0, 3, 1, 0), (0, 2, 1, 2), (0, 2, 1, 0), (2, 0, 3), (3, 3, 0), (4, 1), (2, 1, 3), (3, 2, 0), (4, 3), (4, 0), (2, 1, 2), (4, 2), (2, 0, 2), (0, 3, 1, 3), (0, 2, 1, 3), (0, 0, 1, 0), (3, 0, 0), (0, 1, 1, 0)),
        ((3, 1, 0), (0, 0, 1, 2), (0, 1, 1, 2), (0, 0, 1, 3), (0, 1, 1, 3)),
        (),
    ),
    (
        (),
        (),
        (),
        (),
        (),
        ((1, 0, 0),),
        ((1, 1, 0),),
        (),
        ((1, 1, 1), (1, 0, 1), (1, 1, 2), (1, 0, 2), (1, 1, 3), (1, 0, 3), (0, 0, 0, 2), (0, 1, 0, 2), (0, 0, 0, 1), (0, 0, 0, 3), (0, 0, 1, 2), (0, 3, 0, 2), (0, 2, 0, 2), (0, 1, 0, 3), (0, 1, 0, 1), (0, 1, 1, 2), (0, 3, 0, 3), (0, 2, 0, 3), (0, 3, 0, 1), (0, 3, 1, 2), (0, 2, 0, 1), (0, 2, 1, 2), (3, 3, 0), (0, 0, 0, 0), (3, 2, 0), (3, 3, 1), (0, 1, 0, 0), (0, 3, 0, 0), (0, 2, 0, 0), (3, 2, 1), (0, 3, 1, 1), (2, 2, 3), (0, 2, 1, 1), (0, 3, 1, 3), (0, 2, 1, 3), (2, 3, 3), (4, 2), (3, 0, 0), (4, 1), (4, 3), (4, 0), (3, 1, 0), (0, 3, 1, 0), (0, 2, 1, 0), (3, 1, 1), (2, 0, 3), (3, 0, 1), (0, 0, 1, 1), (0, 0, 1, 3), (2, 1, 3), (0, 1, 1, 1), (0, 1, 1, 3)),
        ((0, 0, 1, 0), (0, 1, 1, 0)),
        (),
    ),
    (
        (),
        (),
        (),
        (),
        (),
        ((1, 0, 0),),
        ((1, 1, 0),),
        (),
        ((1, 1, 1), (1, 0, 1), (3, 3, 0), (3, 2, 0), (3, 3, 1), (1, 1, 2), (1, 0, 2), (3, 2, 1), (1, 1, 3), (3, 3, 2), (1, 0, 3), (3, 2, 2), (0, 0, 0, 3), (0, 1, 0, 3), (0, 0, 1, 3), (0, 0, 0, 2), (0, 3, 0, 3), (0, 1, 1, 3), (0, 2, 0, 3), (0, 3, 1, 3), (0, 1, 0, 2), (0, 2, 1, 3), (0, 3, 0, 2), (0, 2, 0, 2), (3, 0, 0), (3, 1, 0), (0, 0, 0, 1), (0, 1, 0, 1), (3, 1, 1), (0, 3, 0, 1), (3, 0, 1), (0, 3, 1, 2), (0, 2, 0, 1), (0, 2, 1, 2), (3, 1, 2), (3, 0, 2), (0, 0, 0, 0), (4, 1), (0, 1, 0, 0), (0, 3, 0, 0), (4, 0), (0, 2, 0, 0), (0, 3, 1, 1), (4, 2), (0, 2, 1, 1), (0, 0, 1, 2), (0, 1, 1, 2)),
        ((4, 3), (0, 3, 1, 0), (0, 0, 1, 1), (0, 2, 1, 0), (0, 1, 1, 1), (0, 0, 1, 0), (0, 1, 1, 0)),
        (),
    ),
)


def mesh_kernel(
    n,
    sections,
    x_hbm,
    route_a_hbm,
    prob_a_hbm,
    route_b_hbm,
    prob_b_hbm,
    wg_hbm,
    wu_hbm,
    g_hbm,
    u_hbm,
    dh_hbm,
    hidden_ref,
    gx_ref,
    gp_ref,
    route_a_ref,
    prob_a_ref,
    route_b_ref,
    prob_b_ref,
    wg,
    wu,
    g_buf,
    u_buf,
    dh_buf,
    d_gate,
    d_up,
    rows,
    dx,
    in_up,
    in_down,
    in_y,
    fin_in,
    tabs,
    dps,
    dps_up,
    dps_down,
    dps_over,
    load_sem,
    weight_sem,
    shift_send,
    tab_send,
    tab_recv,
    dps_send,
    dps_recv,
    ag_send,
    ag_recv,
    up_send,
    up_recv,
    down_send,
    down_recv,
    y_send,
    y_recv,
    fin_send,
    fin_recv,
):
    tok, width = x_hbm.shape
    units = wg.shape[1]
    pieces = pieces_of(width)
    nz = n // ROWS_Y
    sec = lax.axis_index("pipe")
    me = lax.axis_index("expert")
    z, y = lax.div(me, ROWS_Y), lax.rem(me, ROWS_Y)
    after = lax.rem(sec + 1, sections)
    before = lax.rem(sec + sections - 1, sections)
    across = me + 1 - 2 * y
    top = nz - 1

    loads = [
        pltpu.make_async_copy(src, dst, load_sem.at[i])
        for i, (src, dst) in enumerate(
            (
                (route_a_hbm, route_a_ref),
                (prob_a_hbm, prob_a_ref),
                (route_b_hbm, route_b_ref),
                (prob_b_hbm, prob_b_ref),
                (g_hbm, g_buf),
                (u_hbm, u_buf),
                (dh_hbm, dh_buf),
            )
        )
    ]
    for load in loads:
        load.start()

    barrier = pltpu.get_barrier_semaphore()

    def greet(peer):
        pl.semaphore_signal(barrier, inc=1, device_id=peer, device_id_type=MESH)

    for peer in ((after, me), (before, me)):
        greet(peer)
    for section in (sec, after, before):
        greet((section, across))

        @pl.when(z < top)
        def _():
            greet((section, me + ROWS_Y))

        @pl.when(z > 0)
        def _():
            greet((section, me - ROWS_Y))

    weights = {}
    for c in [c for what, c in COMPUTE if what == 1]:
        start, size, _ = pieces[c]
        span = pl.ds(start, size)
        weights[c] = [
            pltpu.make_async_copy(src.at[span, :], dst.at[span, :], weight_sem.at[i, c])
            for i, (src, dst) in enumerate(((wg_hbm, wg), (wu_hbm, wu)))
        ]
        for load in weights[c]:
            load.start()

    def cols(c):
        start, size, _ = pieces[c]
        return pl.ds(start, size)

    last = len(pieces) - 1
    for load in loads[:2]:
        load.wait()
    route_a = route_a_ref[...]
    prob_a = prob_a_ref[...]
    by_expert = jnp.concatenate(
        [
            jnp.sum(jnp.where(route_a == e, prob_a, 0), axis=0, keepdims=True)
            for e in range(tabs.shape[1])
        ],
        axis=0,
    )
    tabs[me] = jnp.zeros(tabs.shape[1:], tabs.dtype)
    tabs[me, :, 0:tok] = by_expert.astype(jnp.float32).astype(jnp.bfloat16)

    pl.semaphore_wait(
        barrier,
        5 + 3 * jnp.where(z < top, 1, 0) + 3 * jnp.where(z > 0, 1, 0),
    )

    for c in range(len(pieces)):
        if pieces[c][2]:

            @pl.when(z == 0)
            def _():
                fin_in[1, :, cols(c)] = jnp.zeros((tok, pieces[c][1]), fin_in.dtype)

            @pl.when(z == top)
            def _():
                fin_in[2, :, cols(c)] = jnp.zeros((tok, pieces[c][1]), fin_in.dtype)

    started = []

    def remote(src, dst, send_sem, recv_sem, device):
        return pltpu.make_async_remote_copy(
            src_ref=src,
            dst_ref=dst,
            send_sem=send_sem,
            recv_sem=recv_sem,
            device_id=device,
            device_id_type=MESH,
        )

    def arrived(dst, recv_sem):
        remote(dst, dst, recv_sem, recv_sem, (sec, across)).wait_recv()

    def at(zz):
        return pl.when(z == zz)

    UP, DOWN, OVER = 0, 1, 2

    def toward(way):
        return (sec, (me + ROWS_Y, me - ROWS_Y, across)[way])

    def post(zz, copy):
        remote(*copy()).start()
        started.append((zz, copy))

    def neighbours():
        yield None, OVER, across, 1
        for zz in range(nz):
            if zz < top:
                yield zz, UP, me + ROWS_Y, 0
            if zz > 0:
                yield zz, DOWN, me - ROWS_Y, 0

    def first(zz, way, there, v, c):
        def copy():
            if c is None:
                held = tabs.at[me]
                return held, held, tab_send.at[0, z, way], tab_recv.at[v, z], (sec, there)
            span = cols(c)
            held = rows.at[me, :, span]
            return x_hbm.at[:, span], held, shift_send.at[c, way], ag_recv.at[c, v, z], (after, there)

        post(zz, copy)

    for c in [*range(len(pieces)), None]:
        for zz, way, there, v in neighbours():
            if zz is None:
                first(zz, way, there, v, c)
            else:

                @at(zz)
                def _():
                    first(zz, way, there, v, c)

        if c is not None:
            post(
                None,
                lambda c=c: (
                    x_hbm.at[:, cols(c)],
                    rows.at[me, :, cols(c)],
                    shift_send.at[c, 3],
                    ag_recv.at[c, 0, z],
                    (after, me),
                ),
            )

    def expert_at(zz, v):
        return ROWS_Y * zz + (y if v == 0 else 1 - y)

    def ways_of(zz, c, v, zs):
        z_first = pieces[c][2]
        ways = []
        if v == 0 and zs == zz:
            return ways
        if zs <= zz and zz < top and not (z_first and v == 1):
            ways.append(UP)
        if zs >= zz and zz > 0 and not (z_first and v == 1):
            ways.append(DOWN)
        if v == 0 and z_first:
            ways.append(OVER)
        return ways

    def spread_block(zz, c, v, zs):
        block = expert_at(zs, v)
        arrived(rows.at[block, :, cols(c)], ag_recv.at[c, v, zs])
        with_table = c == last and not (v == 0 and zs == zz)
        if with_table:
            arrived(tabs.at[block], tab_recv.at[v, zs])
        for way in ways_of(zz, c, v, zs):

            def copy(way=way):
                held = rows.at[expert_at(zs, v), :, cols(c)]
                there = 1 if way == OVER else v
                recv = ag_recv.at[c, there, zs]
                return held, held, ag_send.at[c, v, zs, way], recv, toward(way)

            post(zz, copy)
            if with_table:

                def small(way=way):
                    held = tabs.at[expert_at(zs, v)]
                    recv = tab_recv.at[1 if way == OVER else v, zs]
                    return held, held, tab_send.at[v, zs, way], recv, toward(way)

                post(zz, small)

    def backward_rows(j):
        span = pl.ds(j * tok, tok)
        g_val = g_buf[span, :].astype(jnp.float32)
        u_val = u_buf[span, :].astype(jnp.float32)
        dh_val = dh_buf[span, :].astype(jnp.float32)
        p_val = to_column(prob_b_ref[pl.ds(j, 1), :].astype(jnp.float32))
        sigma = jax.nn.sigmoid(g_val)
        active = g_val * sigma
        scaled = dh_val * p_val
        d_up[span, :] = (scaled * active).astype(jnp.bfloat16)
        d_gate[span, :] = (scaled * u_val * sigma * (1.0 + g_val * (1.0 - sigma))).astype(
            jnp.bfloat16
        )
        column = jnp.sum(dh_val * active * u_val, axis=1, keepdims=True)
        row = to_row(column)
        line = lax.broadcasted_iota(jnp.int32, (dps.shape[1], tok), 0)
        dps[j] = jnp.zeros(dps.shape[1:], dps.dtype)
        dps[j, :, 0:tok] = jnp.where(line == me, row, 0.0).astype(jnp.bfloat16)

    contract = (((1,), (1,)), ((), ()))

    def gradient(c):
        for load in weights[c]:
            load.wait()
        span = cols(c)
        out = lax.dot_general(
            d_gate[...], wg[span, :], contract, preferred_element_type=jnp.float32
        ) + lax.dot_general(d_up[...], wu[span, :], contract, preferred_element_type=jnp.float32)
        dx[:, :, span] = out.reshape(n, tok, out.shape[1]).astype(jnp.bfloat16)

    def f32(ref_value):
        return ref_value.astype(jnp.float32)

    def trade(zz, c, zt):
        post(
            zz,
            lambda: (
                dx.at[expert_at(zt, 1), :, cols(c)],
                in_y.at[zt, :, cols(c)],
                y_send.at[c, zt],
                y_recv.at[c, zt],
                toward(OVER),
            ),
        )

    def pass_on(zz, c, zt, way):
        z_first = pieces[c][2]
        inbox = in_up if way == UP else in_down
        send_sem, recv_sem = (up_send, up_recv) if way == UP else (down_send, down_recv)
        begins = zz == 0 if way == UP else zz == top
        if z_first:
            here = expert_at(zt, 0)
            total = f32(dx[here, :, cols(c)])
            arrived(in_y.at[zt, :, cols(c)], y_recv.at[c, zt])
            total = total + f32(in_y[zt, :, cols(c)])
            if not begins:
                arrived(inbox.at[here, :, cols(c)], recv_sem.at[c, zt])
                total = total + f32(inbox[here, :, cols(c)])
            dx[here, :, cols(c)] = total.astype(jnp.bfloat16)
        else:
            pair = pl.ds(ROWS_Y * zt, ROWS_Y)
            if not begins:
                arrived(inbox.at[pair, :, cols(c)], recv_sem.at[c, zt])
                total = f32(dx[pair, :, cols(c)]) + f32(inbox[pair, :, cols(c)])
                dx[pair, :, cols(c)] = total.astype(jnp.bfloat16)
                if c == last:
                    small_in = dps_up if way == UP else dps_down
                    arrived(small_in.at[pair], dps_recv.at[way, zt])
                    dps[pair] = (f32(dps[pair]) + f32(small_in[pair])).astype(jnp.bfloat16)
        def copy():
            block = expert_at(zt, 0) if z_first else pl.ds(ROWS_Y * zt, ROWS_Y)
            src, dst = dx.at[block, :, cols(c)], inbox.at[block, :, cols(c)]
            if z_first and abs(zt - zz) == 1:
                there = (before, toward(way)[1])
                return src, fin_in.at[1 + way, :, cols(c)], fin_send.at[c, 1 + way], fin_recv.at[c, 1 + way], there
            return src, dst, send_sem.at[c, zt], recv_sem.at[c, zt], toward(way)

        post(zz, copy)
        if c == last:

            def small():
                pair = pl.ds(ROWS_Y * zt, ROWS_Y)
                dst = (dps_up if way == UP else dps_down).at[pair]
                return dps.at[pair], dst, dps_send.at[way, zt], dps_recv.at[way, zt], toward(way)

            post(zz, small)

    def line_total(zz, c, block):
        total = f32(dx[block, :, cols(c)])
        if zz > 0:
            total = total + f32(in_up[block, :, cols(c)])
        if zz < top:
            total = total + f32(in_down[block, :, cols(c)])
        return total

    def own_line(zz, c):
        z_first = pieces[c][2]
        own, other = expert_at(zz, 0), expert_at(zz, 1)
        if z_first:
            arrived(in_y.at[zz, :, cols(c)], y_recv.at[c, zz])
            total = f32(dx[own, :, cols(c)]) + f32(in_y[zz, :, cols(c)])
            dx[own, :, cols(c)] = total.astype(jnp.bfloat16)
        else:
            pair = pl.ds(ROWS_Y * zz, ROWS_Y)
            if zz > 0:
                arrived(in_up.at[pair, :, cols(c)], up_recv.at[c, zz])
            if zz < top:
                arrived(in_down.at[pair, :, cols(c)], down_recv.at[c, zz])
            dx[other, :, cols(c)] = line_total(zz, c, other).astype(jnp.bfloat16)
            post(
                zz,
                lambda: (
                    dx.at[expert_at(zz, 1), :, cols(c)],
                    fin_in.at[1, :, cols(c)],
                    fin_send.at[c, 1],
                    fin_recv.at[c, 1],
                    (before, across),
                ),
            )
            if c == last:
                small = f32(dps[pair])
                if zz > 0:
                    arrived(dps_up.at[pair], dps_recv.at[UP, zz])
                    small = small + f32(dps_up[pair])
                if zz < top:
                    arrived(dps_down.at[pair], dps_recv.at[DOWN, zz])
                    small = small + f32(dps_down[pair])
                dps[pair] = small.astype(jnp.bfloat16)
                post(
                    zz,
                    lambda: (
                        dps.at[expert_at(zz, 1)],
                        dps_over,
                        dps_send.at[OVER, zz],
                        dps_recv.at[OVER, zz],
                        toward(OVER),
                    ),
                )
            dx[own, :, cols(c)] = line_total(zz, c, own).astype(jnp.bfloat16)
        post(
            zz,
            lambda: (
                dx.at[expert_at(zz, 0), :, cols(c)],
                fin_in.at[0, :, cols(c)],
                fin_send.at[c, 0],
                fin_recv.at[c, 0],
                (before, me),
            ),
        )

    group = n // 2
    near = lax.div(z, nz // 2)

    def hidden_part(half, k):
        part = units // PARTS
        span = pl.ds(k * part, part)
        blocks = pl.ds(half * group, group)
        tokens = rows[blocks, :, pl.ds(0, width)].reshape(group * tok, width)
        gate = jnp.dot(tokens, wg[:, span], preferred_element_type=jnp.float32)
        up = jnp.dot(tokens, wu[:, span], preferred_element_type=jnp.float32)
        table = tabs[blocks, :, 0:tok].astype(jnp.float32)
        mine = lax.broadcasted_iota(jnp.int32, table.shape, 1) == me
        table = jnp.sum(jnp.where(mine, table, 0.0), axis=1) / 256.0
        scale = jnp.concatenate([to_column(table[j : j + 1, :]) for j in range(group)], axis=0)
        lines = pl.ds(pl.multiple_of(half * (group * tok), group * tok), group * tok)
        hidden_ref[lines, span] = (scale * jax.nn.silu(gate) * up).astype(jnp.bfloat16)

    def load_saved():
        for load in loads[3:]:
            load.wait()

    def pick():
        loads[2].wait()
        arrived(dps_over, dps_recv.at[OVER, z])
        by_slot = f32(dps[me]) + f32(dps_over[...])
        route_b = route_b_ref[...]
        picked = jnp.zeros(route_b.shape, jnp.float32)
        for e in range(n):
            picked = picked + jnp.where(route_b == e, by_slot[e : e + 1, 0:tok], 0.0)
        gp_ref[...] = picked.astype(jnp.bfloat16)

    def step(zz, what, c, *rest):
        if what == 0:
            spread_block(zz, c, *rest)
        elif what == 1:
            trade(zz, c, *rest)
        elif what == 4:
            own_line(zz, c)
        else:
            pass_on(zz, c, *rest, UP if what == 2 else DOWN)

    def work(what, k):
        share = n // sum(1 for kind, _ in COMPUTE if kind == 0)
        if what == 0:
            if k == 0:
                load_saved()
            for j in range(k * share, (k + 1) * share):
                backward_rows(j)
        elif what == 1:
            gradient(k)
        else:
            for part in range(PARTS):
                hidden_part(near if k == 0 else 1 - near, part)

    for i in range(len(COMPUTE) + 1):
        for zz in range(nz):
            if ORDERS[zz][i]:

                @at(zz)
                def _():
                    for each in ORDERS[zz][i]:
                        step(zz, *each)

        if i < len(COMPUTE):
            work(*COMPUTE[i])

    pick()
    for c in range(len(pieces)):
        span = cols(c)
        arrived(fin_in.at[0, :, span], fin_recv.at[c, 0])
        if pieces[c][2]:

            @pl.when(z > 0)
            def _():
                arrived(fin_in.at[1, :, span], fin_recv.at[c, 1])

            @pl.when(z < top)
            def _():
                arrived(fin_in.at[2, :, span], fin_recv.at[c, 2])

            total = f32(fin_in[0, :, span]) + f32(fin_in[1, :, span]) + f32(fin_in[2, :, span])
        else:
            arrived(fin_in.at[1, :, span], fin_recv.at[c, 1])
            total = f32(fin_in[0, :, span]) + f32(fin_in[1, :, span])
        gx_ref[:, span] = total.astype(jnp.bfloat16)
    for zz in [None, *range(nz)]:
        copies = [copy for where, copy in started if where == zz]
        if zz is None:
            for copy in copies:
                remote(*copy()).wait_send()
        else:

            @at(zz)
            def _():
                for copy in copies:
                    remote(*copy()).wait_send()


def put_kernel(a_ref, b_ref, c_ref, a_out, b_out, c_out, sem):
    held = ((a_ref, a_out), (b_ref, b_out), (c_ref, c_out))
    puts = [pltpu.make_async_copy(src, dst, sem.at[i]) for i, (src, dst) in enumerate(held)]
    for put in puts:
        put.start()
    for put in puts:
        put.wait()


def full_routing(
    x_prev_a,
    route_a,
    prob_a,
    w_gate,
    w_up,
    route_b,
    prob_b,
    saved_gate_b,
    saved_up_b,
    grad_hidden_b,
):
    n = lax.axis_size("expert")
    sections = lax.axis_size("pipe")
    tok, width = x_prev_a.shape[1:]
    top_k = route_a.shape[2]
    units = saved_gate_b.shape[4]
    slots = n * tok
    nz = n // ROWS_Y
    count = len(pieces_of(width))
    small = (16 * pl.cdiv(n, 16), LANES * pl.cdiv(tok, LANES))
    bf16 = jnp.bfloat16
    dma = pltpu.SemaphoreType.DMA
    any_ = pl.BlockSpec(memory_space=pl.ANY)
    vmem = pl.BlockSpec(memory_space=pltpu.VMEM)
    hidden, grad_x, grad_prob = pl.pallas_call(
        functools.partial(mesh_kernel, n, sections),
        out_shape=(
            pltpu.VMEM((slots, units), bf16),
            pltpu.VMEM((tok, width), bf16),
            pltpu.VMEM((top_k, tok), bf16),
        ),
        in_specs=[any_] * 10,
        out_specs=(vmem,) * 3,
        scratch_shapes=[
            pltpu.VMEM((top_k, tok), jnp.int32),
            pltpu.VMEM((top_k, tok), jnp.int32),
            pltpu.VMEM((top_k, tok), jnp.int32),
            pltpu.VMEM((n, tok), bf16),
            pltpu.VMEM((width, units), bf16),
            pltpu.VMEM((width, units), bf16),
            pltpu.VMEM((slots, units), bf16),
            pltpu.VMEM((slots, units), bf16),
            pltpu.VMEM((slots, units), bf16),
            pltpu.VMEM((slots, units), bf16),
            pltpu.VMEM((slots, units), bf16),
            pltpu.VMEM((n, tok, width), bf16),
            pltpu.VMEM((n, tok, width), bf16),
            pltpu.VMEM((n, tok, width), bf16),
            pltpu.VMEM((n, tok, width), bf16),
            pltpu.VMEM((nz, tok, width), bf16),
            pltpu.VMEM((3, tok, width), bf16),
            pltpu.VMEM((n, *small), bf16),
            pltpu.VMEM((n, *small), bf16),
            pltpu.VMEM((n, *small), bf16),
            pltpu.VMEM((n, *small), bf16),
            pltpu.VMEM(small, bf16),
            dma((7,)),
            dma((2, count)),
            dma((count, 4)),
            dma((2, nz, 3)),
            dma((2, nz)),
            dma((3, nz)),
            dma((3, nz)),
            dma((count, 2, nz, 3)),
            dma((count, 2, nz)),
            dma((count, nz)),
            dma((count, nz)),
            dma((count, nz)),
            dma((count, nz)),
            dma((count, nz)),
            dma((count, nz)),
            dma((count, 3)),
            dma((count, 3)),
        ],
        compiler_params=pltpu.CompilerParams(
            collective_id=0, has_side_effects=True, vmem_limit_bytes=VMEM_BYTES
        ),
        name="mesh",
    )(
        x_prev_a[0],
        route_a[0].T,
        prob_a[0].T,
        route_b[0].T,
        prob_b[0, 0],
        w_gate[0],
        w_up[0],
        saved_gate_b.reshape(slots, units),
        saved_up_b.reshape(slots, units),
        grad_hidden_b.reshape(slots, units),
    )
    results = (hidden, grad_x, grad_prob)
    hidden, grad_x, grad_prob = pl.pallas_call(
        put_kernel,
        out_shape=tuple(jax.ShapeDtypeStruct(a.shape, a.dtype) for a in results),
        in_specs=[any_] * 3,
        out_specs=(any_,) * 3,
        scratch_shapes=[dma((3,))],
        compiler_params=pltpu.CompilerParams(vmem_limit_bytes=1 << 20),
        name="put",
    )(*results)
    return (
        hidden.reshape(1, 1, n, tok, units),
        grad_x[None],
        grad_prob.T[None],
    )


def any_routing(*args):
    tokens, top_k = args[1].shape[1:]
    capacity = args[7].shape[3]
    full = top_k == lax.axis_size("expert") and capacity == tokens
    if full and top_k == 8 == ROWS_Y * len(ORDERS) and lax.axis_size("pipe") > 2:
        return full_routing(*args)
    return per_device(*args)


def solution(mesh):
    return jax.shard_map(
        any_routing,
        mesh=mesh,
        in_specs=(
            P("pipe", "expert", None),
            P("pipe", "expert", None),
            P("pipe", "expert", None),
            P("expert", None, None),
            P("expert", None, None),
            P("pipe", "expert", None),
            P("pipe", "expert", None, None),
            P("pipe", "expert", None, None, None),
            P("pipe", "expert", None, None, None),
            P("pipe", "expert", None, None, None),
        ),
        out_specs=(
            P("pipe", "expert", None, None, None),
            P("pipe", "expert", None),
            P("pipe", "expert", None),
        ),
        check_vma=False,
    )
```

```python
import functools

import jax
import jax.numpy as jnp
from jax import lax
from jax.experimental import pallas as pl
from jax.experimental.pallas import tpu as pltpu
from jax.sharding import PartitionSpec as P


def passed_along(block, axis, distance):
    devices = range(lax.axis_size(axis))
    route = [((i - distance) % len(devices), i) for i in devices]
    return lax.ppermute(block, axis, route)


def slot_choice(route, capacity, experts):
    expert_ids = route[0]
    tok_rows, top_k = expert_ids.shape
    flat_ids = expert_ids.reshape(-1)
    onehot = (flat_ids[:, None] == jnp.arange(experts, dtype=jnp.int32)[None, :]).astype(jnp.int32)
    rows = flat_ids.shape[0]
    earlier = jnp.arange(rows)[:, None] > jnp.arange(rows)[None, :]
    before = jnp.dot(
        earlier.astype(jnp.bfloat16),
        onehot.astype(jnp.bfloat16),
        preferred_element_type=jnp.float32,
    ).astype(jnp.int32)
    slot_rank = jnp.sum(before * onehot, axis=1)
    target = jnp.where(slot_rank < capacity, flat_ids * capacity + slot_rank, -1).reshape(
        tok_rows, top_k
    )
    slot_ids = jnp.arange(experts * capacity, dtype=jnp.int32)
    return (target[:, :, None] == slot_ids[None, None, :]).astype(jnp.float32)


def dispatch_rows(tokens, route, quant, capacity, experts):
    chosen = slot_choice(route, capacity, experts)
    picker = jnp.sum(chosen, axis=1).astype(jnp.bfloat16)
    send_x = jnp.einsum("ts,td->sd", picker, tokens[0], preferred_element_type=jnp.float32).astype(
        jnp.bfloat16
    )
    send_p = (jnp.einsum("tks,tk->s", chosen, quant[0].astype(jnp.float32)) / 256.0).astype(
        jnp.bfloat16
    )
    return (send_x.reshape(experts, capacity, -1), send_p.reshape(experts, capacity))


def per_device(
    x_prev_a,
    route_a,
    prob_a,
    w_gate,
    w_up,
    route_b,
    prob_b,
    saved_gate_b,
    saved_up_b,
    grad_hidden_b,
):
    experts = lax.axis_size("expert")
    capacity = saved_gate_b.shape[3]
    width = x_prev_a.shape[2]
    units = saved_gate_b.shape[4]
    gate_weight = w_gate[0]
    up_weight = w_up[0]
    x_here = passed_along(x_prev_a, "pipe", 1)
    send_x, send_p = dispatch_rows(x_here, route_a, prob_a, capacity, experts)
    recv_x, recv_p = (
        lax.all_to_all(send_x, "expert", split_axis=0, concat_axis=0, tiled=True),
        lax.all_to_all(send_p, "expert", split_axis=0, concat_axis=0, tiled=True),
    )
    rows = recv_x.reshape(-1, width)
    gate = jnp.dot(rows, gate_weight, preferred_element_type=jnp.float32)
    up_proj = jnp.dot(rows, up_weight, preferred_element_type=jnp.float32)
    scale = recv_p.reshape(-1, 1).astype(jnp.float32)
    hidden = (scale * jax.nn.silu(gate) * up_proj).astype(jnp.bfloat16)
    hidden_a = hidden.reshape(1, 1, experts, capacity, units)
    g_val = saved_gate_b[0, 0].reshape(-1, units).astype(jnp.float32)
    u_val = saved_up_b[0, 0].reshape(-1, units).astype(jnp.float32)
    dh_val = grad_hidden_b[0, 0].reshape(-1, units).astype(jnp.float32)
    p_val = prob_b[0, 0].reshape(-1, 1).astype(jnp.float32)
    sigma = jax.nn.sigmoid(g_val)
    active = g_val * sigma
    scaled = dh_val * p_val
    d_up = (scaled * active).astype(jnp.bfloat16)
    d_gate = (scaled * u_val * sigma * (1.0 + g_val * (1.0 - sigma))).astype(jnp.bfloat16)
    slot_dx = (
        jnp.einsum("rh,dh->rd", d_gate, gate_weight, preferred_element_type=jnp.float32)
        + jnp.einsum("rh,dh->rd", d_up, up_weight, preferred_element_type=jnp.float32)
    ).astype(jnp.bfloat16)
    slot_dp = jnp.sum(dh_val * active * u_val, axis=1).astype(jnp.bfloat16)
    back_x, back_p = (
        lax.all_to_all(
            slot_dx.reshape(experts, capacity, width),
            "expert",
            split_axis=0,
            concat_axis=0,
            tiled=True,
        ),
        lax.all_to_all(
            slot_dp.reshape(experts, capacity), "expert", split_axis=0, concat_axis=0, tiled=True
        ),
    )
    chosen_b = slot_choice(route_b, capacity, experts)
    picker_b = jnp.sum(chosen_b, axis=1).astype(jnp.bfloat16)
    grad_tokens = jnp.dot(
        picker_b, back_x.reshape(-1, width), preferred_element_type=jnp.float32
    ).astype(jnp.bfloat16)
    grad_prob = jnp.einsum("tks,s->tk", chosen_b, back_p.reshape(-1).astype(jnp.float32)).astype(
        jnp.bfloat16
    )
    grad_x_b = passed_along(grad_tokens[None], "pipe", -1)
    return (hidden_a, grad_x_b, grad_prob[None])


MESH = pl.DeviceIdType.MESH


def to_column(row):
    size = row.shape[1]
    eye = lax.broadcasted_iota(jnp.int32, (size, size), 0) == lax.broadcasted_iota(
        jnp.int32, (size, size), 1
    )
    return jnp.sum(jnp.where(eye, jnp.broadcast_to(row, (size, size)), 0.0), axis=1, keepdims=True)


def to_row(column):
    size = column.shape[0]
    eye = lax.broadcasted_iota(jnp.int32, (size, size), 0) == lax.broadcasted_iota(
        jnp.int32, (size, size), 1
    )
    return jnp.sum(
        jnp.where(eye, jnp.broadcast_to(column, (size, size)), 0.0), axis=0, keepdims=True
    )


VMEM_BYTES = 62 * 1024 * 1024 + 512 * 1024
LANES = 128
ROWS_Y = 2
PARTS = 3


SHARES = ((6, True), (6, True), (2, False), (2, False))


def pieces_of(width):
    units, whole = width // LANES, sum(share for share, _ in SHARES)
    pieces, start, taken = [], 0, 0
    for share, z_first in SHARES:
        taken += share
        end = units * taken // whole
        pieces.append((start * LANES, (end - start) * LANES, z_first))
        start = end
    return pieces


COMPUTE = ((0, 0), (0, 1), (0, 2), (0, 3), (1, 0), (1, 1), (1, 3), (1, 2), (2, 0), (2, 1))
ORDERS = (
    (
        (),
        (),
        (),
        (),
        (),
        ((1, 0, 3),),
        ((1, 1, 3), (1, 0, 2)),
        ((2, 3, 3), (1, 1, 2), (2, 3, 2), (1, 0, 1)),
        ((1, 0, 0), (1, 1, 1), (1, 1, 0), (2, 2, 3), (2, 2, 2), (2, 3, 1), (2, 2, 1), (0, 0, 0, 0), (0, 1, 0, 0), (0, 0, 1, 0), (0, 3, 0, 0), (0, 2, 0, 0), (0, 1, 1, 0), (0, 0, 0, 1), (0, 3, 1, 0), (0, 2, 1, 0), (0, 1, 0, 1), (2, 0, 3), (0, 3, 0, 1), (0, 2, 0, 1), (2, 1, 3), (2, 0, 2), (0, 0, 0, 2), (0, 3, 1, 1), (2, 1, 2), (0, 1, 0, 2), (0, 2, 1, 1), (0, 3, 0, 2), (2, 0, 1), (0, 2, 0, 2), (4, 0), (2, 1, 1), (4, 1), (0, 0, 0, 3), (0, 1, 0, 3), (0, 3, 0, 3), (0, 2, 0, 3), (0, 0, 1, 1), (0, 3, 1, 2), (0, 1, 1, 1), (0, 2, 1, 2)),
        ((4, 3), (0, 0, 1, 2), (4, 2), (0, 1, 1, 2), (0, 3, 1, 3), (0, 2, 1, 3), (0, 0, 1, 3), (0, 1, 1, 3)),
        (),
    ),
    (
        (),
        (),
        (),
        (),
        (),
        ((1, 0, 3), (1, 0, 0)),
        ((1, 0, 1), (1, 1, 3), (1, 0, 2), (1, 1, 0)),
        ((1, 1, 1), (1, 1, 2)),
        ((0, 0, 0, 1), (0, 1, 0, 1), (0, 0, 0, 0), (0, 0, 1, 1), (0, 3, 0, 1), (0, 1, 0, 0), (0, 2, 0, 1), (0, 3, 0, 0), (0, 0, 0, 2), (0, 1, 1, 1), (0, 2, 0, 0), (0, 3, 1, 1), (0, 1, 0, 2), (0, 2, 1, 1), (0, 3, 0, 2), (2, 3, 3), (0, 2, 0, 2), (2, 3, 2), (2, 2, 3), (2, 2, 2), (0, 0, 0, 3), (0, 1, 0, 3), (0, 3, 0, 3), (0, 2, 0, 3), (0, 3, 1, 2), (0, 3, 1, 0), (0, 2, 1, 2), (0, 2, 1, 0), (4, 0), (2, 0, 3), (3, 3, 0), (3, 2, 0), (2, 1, 3), (4, 2), (2, 0, 2), (4, 1), (4, 3), (0, 3, 1, 3), (0, 2, 1, 3), (2, 1, 2), (0, 0, 1, 0), (3, 0, 0), (0, 1, 1, 0)),
        ((3, 1, 0), (0, 0, 1, 2), (0, 1, 1, 2), (0, 0, 1, 3), (0, 1, 1, 3)),
        (),
    ),
    (
        (),
        (),
        (),
        (),
        (),
        ((1, 0, 0),),
        ((1, 1, 0),),
        ((1, 0, 1), (1, 0, 3), (1, 1, 1)),
        ((1, 0, 2), (1, 1, 3), (1, 1, 2), (0, 0, 0, 2), (0, 1, 0, 2), (0, 0, 0, 1), (0, 0, 0, 3), (0, 0, 1, 2), (0, 3, 0, 2), (0, 2, 0, 2), (0, 1, 0, 3), (0, 1, 0, 1), (0, 1, 1, 2), (0, 3, 0, 3), (0, 2, 0, 3), (0, 3, 0, 1), (0, 3, 1, 2), (0, 2, 0, 1), (0, 2, 1, 2), (3, 3, 0), (0, 0, 0, 0), (3, 2, 0), (0, 1, 0, 0), (3, 2, 1), (0, 3, 0, 0), (0, 2, 0, 0), (3, 3, 1), (0, 3, 1, 1), (0, 2, 1, 1), (2, 3, 3), (0, 3, 1, 3), (4, 3), (0, 2, 1, 3), (3, 0, 0), (4, 0), (2, 2, 3), (4, 2), (3, 1, 0), (0, 3, 1, 0), (4, 1), (0, 2, 1, 0), (3, 0, 1), (2, 0, 3), (3, 1, 1), (2, 1, 3), (0, 0, 1, 3), (0, 0, 1, 1), (0, 1, 1, 1), (0, 1, 1, 3)),
        ((0, 0, 1, 0), (0, 1, 1, 0)),
        (),
    ),
    (
        (),
        (),
        (),
        (),
        (),
        ((1, 0, 0),),
        ((1, 1, 0),),
        ((1, 0, 1), (1, 1, 1), (3, 3, 0)),
        ((3, 2, 0), (1, 0, 2), (3, 2, 1), (1, 0, 3), (1, 1, 2), (3, 3, 1), (1, 1, 3), (3, 2, 2), (3, 3, 2), (0, 0, 0, 3), (0, 1, 0, 3), (0, 0, 1, 3), (0, 0, 0, 2), (0, 3, 0, 3), (0, 1, 1, 3), (0, 2, 0, 3), (0, 3, 1, 3), (0, 1, 0, 2), (0, 2, 1, 3), (0, 3, 0, 2), (0, 2, 0, 2), (3, 0, 0), (3, 1, 0), (0, 0, 0, 1), (3, 0, 1), (0, 1, 0, 1), (0, 3, 0, 1), (3, 1, 1), (0, 3, 1, 2), (0, 2, 0, 1), (0, 2, 1, 2), (3, 0, 2), (0, 0, 0, 0), (4, 0), (3, 1, 2), (0, 1, 0, 0), (0, 3, 0, 0), (0, 2, 0, 0), (4, 1), (0, 3, 1, 1), (0, 2, 1, 1), (0, 0, 1, 2), (4, 3), (0, 1, 1, 2)),
        ((4, 2), (0, 3, 1, 0), (0, 0, 1, 1), (0, 2, 1, 0), (0, 1, 1, 1), (0, 0, 1, 0), (0, 1, 1, 0)),
        (),
    ),
)


def mesh_kernel(
    n,
    sections,
    x_hbm,
    route_a_hbm,
    prob_a_hbm,
    route_b_hbm,
    prob_b_hbm,
    wg_hbm,
    wu_hbm,
    g_hbm,
    u_hbm,
    dh_hbm,
    hidden_ref,
    gx_ref,
    gp_ref,
    route_a_ref,
    prob_a_ref,
    route_b_ref,
    prob_b_ref,
    wg,
    wu,
    g_buf,
    u_buf,
    dh_buf,
    d_gate,
    d_up,
    rows,
    dx,
    in_up,
    in_down,
    in_y,
    fin_in,
    tabs,
    dps,
    dps_up,
    dps_down,
    dps_over,
    load_sem,
    weight_sem,
    shift_send,
    tab_send,
    tab_recv,
    dps_send,
    dps_recv,
    ag_send,
    ag_recv,
    up_send,
    up_recv,
    down_send,
    down_recv,
    y_send,
    y_recv,
    fin_send,
    fin_recv,
):
    tok, width = x_hbm.shape
    units = wg.shape[1]
    pieces = pieces_of(width)
    nz = n // ROWS_Y
    sec = lax.axis_index("pipe")
    me = lax.axis_index("expert")
    z, y = lax.div(me, ROWS_Y), lax.rem(me, ROWS_Y)
    after = lax.rem(sec + 1, sections)
    before = lax.rem(sec + sections - 1, sections)
    across = me + 1 - 2 * y
    top = nz - 1

    loads = [
        pltpu.make_async_copy(src, dst, load_sem.at[i])
        for i, (src, dst) in enumerate(
            (
                (route_a_hbm, route_a_ref),
                (prob_a_hbm, prob_a_ref),
                (route_b_hbm, route_b_ref),
                (prob_b_hbm, prob_b_ref),
                (g_hbm, g_buf),
                (u_hbm, u_buf),
                (dh_hbm, dh_buf),
            )
        )
    ]
    for load in loads:
        load.start()

    barrier = pltpu.get_barrier_semaphore()

    def greet(peer):
        pl.semaphore_signal(barrier, inc=1, device_id=peer, device_id_type=MESH)

    for peer in ((after, me), (before, me)):
        greet(peer)
    for section in (sec, after, before):
        greet((section, across))

        @pl.when(z < top)
        def _():
            greet((section, me + ROWS_Y))

        @pl.when(z > 0)
        def _():
            greet((section, me - ROWS_Y))

    weights = {}
    for c in [c for what, c in COMPUTE if what == 1]:
        start, size, _ = pieces[c]
        span = pl.ds(start, size)
        weights[c] = [
            pltpu.make_async_copy(src.at[span, :], dst.at[span, :], weight_sem.at[i, c])
            for i, (src, dst) in enumerate(((wg_hbm, wg), (wu_hbm, wu)))
        ]
        for load in weights[c]:
            load.start()

    def cols(c):
        start, size, _ = pieces[c]
        return pl.ds(start, size)

    last = len(pieces) - 1
    for load in loads[:2]:
        load.wait()
    route_a = route_a_ref[...]
    prob_a = prob_a_ref[...]
    by_expert = jnp.concatenate(
        [
            jnp.sum(jnp.where(route_a == e, prob_a, 0), axis=0, keepdims=True)
            for e in range(tabs.shape[1])
        ],
        axis=0,
    )
    tabs[me] = jnp.zeros(tabs.shape[1:], tabs.dtype)
    tabs[me, :, 0:tok] = by_expert.astype(jnp.float32).astype(jnp.bfloat16)

    pl.semaphore_wait(
        barrier,
        5 + 3 * jnp.where(z < top, 1, 0) + 3 * jnp.where(z > 0, 1, 0),
    )

    for c in range(len(pieces)):
        if pieces[c][2]:

            @pl.when(z == 0)
            def _():
                fin_in[1, :, cols(c)] = jnp.zeros((tok, pieces[c][1]), fin_in.dtype)

            @pl.when(z == top)
            def _():
                fin_in[2, :, cols(c)] = jnp.zeros((tok, pieces[c][1]), fin_in.dtype)

    started = []

    def remote(src, dst, send_sem, recv_sem, device):
        return pltpu.make_async_remote_copy(
            src_ref=src,
            dst_ref=dst,
            send_sem=send_sem,
            recv_sem=recv_sem,
            device_id=device,
            device_id_type=MESH,
        )

    def arrived(dst, recv_sem):
        remote(dst, dst, recv_sem, recv_sem, (sec, across)).wait_recv()

    def at(zz):
        return pl.when(z == zz)

    UP, DOWN, OVER = 0, 1, 2

    def toward(way):
        return (sec, (me + ROWS_Y, me - ROWS_Y, across)[way])

    def post(zz, copy):
        remote(*copy()).start()
        started.append((zz, copy))

    def neighbours():
        yield None, OVER, across, 1
        for zz in range(nz):
            if zz < top:
                yield zz, UP, me + ROWS_Y, 0
            if zz > 0:
                yield zz, DOWN, me - ROWS_Y, 0

    def first(zz, way, there, v, c):
        def copy():
            if c is None:
                held = tabs.at[me]
                return held, held, tab_send.at[0, z, way], tab_recv.at[v, z], (sec, there)
            span = cols(c)
            held = rows.at[me, :, span]
            return x_hbm.at[:, span], held, shift_send.at[c, way], ag_recv.at[c, v, z], (after, there)

        post(zz, copy)

    for c in [*range(len(pieces)), None]:
        for zz, way, there, v in neighbours():
            if zz is None:
                first(zz, way, there, v, c)
            else:

                @at(zz)
                def _():
                    first(zz, way, there, v, c)

        if c is not None:
            post(
                None,
                lambda c=c: (
                    x_hbm.at[:, cols(c)],
                    rows.at[me, :, cols(c)],
                    shift_send.at[c, 3],
                    ag_recv.at[c, 0, z],
                    (after, me),
                ),
            )

    def expert_at(zz, v):
        return ROWS_Y * zz + (y if v == 0 else 1 - y)

    def ways_of(zz, c, v, zs):
        z_first = pieces[c][2]
        ways = []
        if v == 0 and zs == zz:
            return ways
        if zs <= zz and zz < top and not (z_first and v == 1):
            ways.append(UP)
        if zs >= zz and zz > 0 and not (z_first and v == 1):
            ways.append(DOWN)
        if v == 0 and z_first:
            ways.append(OVER)
        return ways

    def spread_block(zz, c, v, zs):
        block = expert_at(zs, v)
        arrived(rows.at[block, :, cols(c)], ag_recv.at[c, v, zs])
        with_table = c == last and not (v == 0 and zs == zz)
        if with_table:
            arrived(tabs.at[block], tab_recv.at[v, zs])
        for way in ways_of(zz, c, v, zs):

            def copy(way=way):
                held = rows.at[expert_at(zs, v), :, cols(c)]
                there = 1 if way == OVER else v
                recv = ag_recv.at[c, there, zs]
                return held, held, ag_send.at[c, v, zs, way], recv, toward(way)

            post(zz, copy)
            if with_table:

                def small(way=way):
                    held = tabs.at[expert_at(zs, v)]
                    recv = tab_recv.at[1 if way == OVER else v, zs]
                    return held, held, tab_send.at[v, zs, way], recv, toward(way)

                post(zz, small)

    def backward_rows(j):
        span = pl.ds(j * tok, tok)
        g_val = g_buf[span, :].astype(jnp.float32)
        u_val = u_buf[span, :].astype(jnp.float32)
        dh_val = dh_buf[span, :].astype(jnp.float32)
        p_val = to_column(prob_b_ref[pl.ds(j, 1), :].astype(jnp.float32))
        sigma = jax.nn.sigmoid(g_val)
        active = g_val * sigma
        scaled = dh_val * p_val
        d_up[span, :] = (scaled * active).astype(jnp.bfloat16)
        d_gate[span, :] = (scaled * u_val * sigma * (1.0 + g_val * (1.0 - sigma))).astype(
            jnp.bfloat16
        )
        column = jnp.sum(dh_val * active * u_val, axis=1, keepdims=True)
        row = to_row(column)
        line = lax.broadcasted_iota(jnp.int32, (dps.shape[1], tok), 0)
        dps[j] = jnp.zeros(dps.shape[1:], dps.dtype)
        dps[j, :, 0:tok] = jnp.where(line == me, row, 0.0).astype(jnp.bfloat16)

    contract = (((1,), (1,)), ((), ()))

    def gradient(c):
        for load in weights[c]:
            load.wait()
        span = cols(c)
        out = lax.dot_general(
            d_gate[...], wg[span, :], contract, preferred_element_type=jnp.float32
        ) + lax.dot_general(d_up[...], wu[span, :], contract, preferred_element_type=jnp.float32)
        dx[:, :, span] = out.reshape(n, tok, out.shape[1]).astype(jnp.bfloat16)

    def f32(ref_value):
        return ref_value.astype(jnp.float32)

    def trade(zz, c, zt):
        post(
            zz,
            lambda: (
                dx.at[expert_at(zt, 1), :, cols(c)],
                in_y.at[zt, :, cols(c)],
                y_send.at[c, zt],
                y_recv.at[c, zt],
                toward(OVER),
            ),
        )

    def pass_on(zz, c, zt, way):
        z_first = pieces[c][2]
        inbox = in_up if way == UP else in_down
        send_sem, recv_sem = (up_send, up_recv) if way == UP else (down_send, down_recv)
        begins = zz == 0 if way == UP else zz == top
        if z_first:
            here = expert_at(zt, 0)
            total = f32(dx[here, :, cols(c)])
            arrived(in_y.at[zt, :, cols(c)], y_recv.at[c, zt])
            total = total + f32(in_y[zt, :, cols(c)])
            if not begins:
                arrived(inbox.at[here, :, cols(c)], recv_sem.at[c, zt])
                total = total + f32(inbox[here, :, cols(c)])
            dx[here, :, cols(c)] = total.astype(jnp.bfloat16)
        else:
            pair = pl.ds(ROWS_Y * zt, ROWS_Y)
            if not begins:
                arrived(inbox.at[pair, :, cols(c)], recv_sem.at[c, zt])
                total = f32(dx[pair, :, cols(c)]) + f32(inbox[pair, :, cols(c)])
                dx[pair, :, cols(c)] = total.astype(jnp.bfloat16)
                if c == last:
                    small_in = dps_up if way == UP else dps_down
                    arrived(small_in.at[pair], dps_recv.at[way, zt])
                    dps[pair] = (f32(dps[pair]) + f32(small_in[pair])).astype(jnp.bfloat16)
        def copy():
            block = expert_at(zt, 0) if z_first else pl.ds(ROWS_Y * zt, ROWS_Y)
            src, dst = dx.at[block, :, cols(c)], inbox.at[block, :, cols(c)]
            if z_first and abs(zt - zz) == 1:
                there = (before, toward(way)[1])
                return src, fin_in.at[1 + way, :, cols(c)], fin_send.at[c, 1 + way], fin_recv.at[c, 1 + way], there
            return src, dst, send_sem.at[c, zt], recv_sem.at[c, zt], toward(way)

        post(zz, copy)
        if c == last:

            def small():
                pair = pl.ds(ROWS_Y * zt, ROWS_Y)
                dst = (dps_up if way == UP else dps_down).at[pair]
                return dps.at[pair], dst, dps_send.at[way, zt], dps_recv.at[way, zt], toward(way)

            post(zz, small)

    def line_total(zz, c, block):
        total = f32(dx[block, :, cols(c)])
        if zz > 0:
            total = total + f32(in_up[block, :, cols(c)])
        if zz < top:
            total = total + f32(in_down[block, :, cols(c)])
        return total

    def own_line(zz, c):
        z_first = pieces[c][2]
        own, other = expert_at(zz, 0), expert_at(zz, 1)
        if z_first:
            arrived(in_y.at[zz, :, cols(c)], y_recv.at[c, zz])
            total = f32(dx[own, :, cols(c)]) + f32(in_y[zz, :, cols(c)])
            dx[own, :, cols(c)] = total.astype(jnp.bfloat16)
        else:
            pair = pl.ds(ROWS_Y * zz, ROWS_Y)
            if zz > 0:
                arrived(in_up.at[pair, :, cols(c)], up_recv.at[c, zz])
            if zz < top:
                arrived(in_down.at[pair, :, cols(c)], down_recv.at[c, zz])
            dx[other, :, cols(c)] = line_total(zz, c, other).astype(jnp.bfloat16)
            post(
                zz,
                lambda: (
                    dx.at[expert_at(zz, 1), :, cols(c)],
                    fin_in.at[1, :, cols(c)],
                    fin_send.at[c, 1],
                    fin_recv.at[c, 1],
                    (before, across),
                ),
            )
            if c == last:
                small = f32(dps[pair])
                if zz > 0:
                    arrived(dps_up.at[pair], dps_recv.at[UP, zz])
                    small = small + f32(dps_up[pair])
                if zz < top:
                    arrived(dps_down.at[pair], dps_recv.at[DOWN, zz])
                    small = small + f32(dps_down[pair])
                dps[pair] = small.astype(jnp.bfloat16)
                post(
                    zz,
                    lambda: (
                        dps.at[expert_at(zz, 1)],
                        dps_over,
                        dps_send.at[OVER, zz],
                        dps_recv.at[OVER, zz],
                        toward(OVER),
                    ),
                )
            dx[own, :, cols(c)] = line_total(zz, c, own).astype(jnp.bfloat16)
        post(
            zz,
            lambda: (
                dx.at[expert_at(zz, 0), :, cols(c)],
                fin_in.at[0, :, cols(c)],
                fin_send.at[c, 0],
                fin_recv.at[c, 0],
                (before, me),
            ),
        )

    group = n // 2
    near = lax.div(z, nz // 2)

    def hidden_part(half, k):
        part = units // PARTS
        span = pl.ds(k * part, part)
        blocks = pl.ds(half * group, group)
        tokens = rows[blocks, :, pl.ds(0, width)].reshape(group * tok, width)
        gate = jnp.dot(tokens, wg[:, span], preferred_element_type=jnp.float32)
        up = jnp.dot(tokens, wu[:, span], preferred_element_type=jnp.float32)
        table = tabs[blocks, :, 0:tok].astype(jnp.float32)
        mine = lax.broadcasted_iota(jnp.int32, table.shape, 1) == me
        table = jnp.sum(jnp.where(mine, table, 0.0), axis=1) / 256.0
        scale = jnp.concatenate([to_column(table[j : j + 1, :]) for j in range(group)], axis=0)
        lines = pl.ds(pl.multiple_of(half * (group * tok), group * tok), group * tok)
        hidden_ref[lines, span] = (scale * jax.nn.silu(gate) * up).astype(jnp.bfloat16)

    def load_saved():
        for load in loads[3:]:
            load.wait()

    def pick():
        loads[2].wait()
        arrived(dps_over, dps_recv.at[OVER, z])
        by_slot = f32(dps[me]) + f32(dps_over[...])
        route_b = route_b_ref[...]
        picked = jnp.zeros(route_b.shape, jnp.float32)
        for e in range(n):
            picked = picked + jnp.where(route_b == e, by_slot[e : e + 1, 0:tok], 0.0)
        gp_ref[...] = picked.astype(jnp.bfloat16)

    def step(zz, what, c, *rest):
        if what == 0:
            spread_block(zz, c, *rest)
        elif what == 1:
            trade(zz, c, *rest)
        elif what == 4:
            own_line(zz, c)
        else:
            pass_on(zz, c, *rest, UP if what == 2 else DOWN)

    def work(what, k):
        share = n // sum(1 for kind, _ in COMPUTE if kind == 0)
        if what == 0:
            if k == 0:
                load_saved()
            for j in range(k * share, (k + 1) * share):
                backward_rows(j)
        elif what == 1:
            gradient(k)
        else:
            for part in range(PARTS):
                hidden_part(near if k == 0 else 1 - near, part)

    for i in range(len(COMPUTE) + 1):
        for zz in range(nz):
            if ORDERS[zz][i]:

                @at(zz)
                def _():
                    for each in ORDERS[zz][i]:
                        step(zz, *each)

        if i < len(COMPUTE):
            work(*COMPUTE[i])

    pick()
    for c in range(len(pieces)):
        span = cols(c)
        arrived(fin_in.at[0, :, span], fin_recv.at[c, 0])
        if pieces[c][2]:

            @pl.when(z > 0)
            def _():
                arrived(fin_in.at[1, :, span], fin_recv.at[c, 1])

            @pl.when(z < top)
            def _():
                arrived(fin_in.at[2, :, span], fin_recv.at[c, 2])

            total = f32(fin_in[0, :, span]) + f32(fin_in[1, :, span]) + f32(fin_in[2, :, span])
        else:
            arrived(fin_in.at[1, :, span], fin_recv.at[c, 1])
            total = f32(fin_in[0, :, span]) + f32(fin_in[1, :, span])
        gx_ref[:, span] = total.astype(jnp.bfloat16)
    for zz in [None, *range(nz)]:
        copies = [copy for where, copy in started if where == zz]
        if zz is None:
            for copy in copies:
                remote(*copy()).wait_send()
        else:

            @at(zz)
            def _():
                for copy in copies:
                    remote(*copy()).wait_send()


def put_kernel(a_ref, b_ref, c_ref, a_out, b_out, c_out, sem):
    held = ((a_ref, a_out), (b_ref, b_out), (c_ref, c_out))
    puts = [pltpu.make_async_copy(src, dst, sem.at[i]) for i, (src, dst) in enumerate(held)]
    for put in puts:
        put.start()
    for put in puts:
        put.wait()


def full_routing(
    x_prev_a,
    route_a,
    prob_a,
    w_gate,
    w_up,
    route_b,
    prob_b,
    saved_gate_b,
    saved_up_b,
    grad_hidden_b,
):
    n = lax.axis_size("expert")
    sections = lax.axis_size("pipe")
    tok, width = x_prev_a.shape[1:]
    top_k = route_a.shape[2]
    units = saved_gate_b.shape[4]
    slots = n * tok
    nz = n // ROWS_Y
    count = len(pieces_of(width))
    small = (16 * pl.cdiv(n, 16), LANES * pl.cdiv(tok, LANES))
    bf16 = jnp.bfloat16
    dma = pltpu.SemaphoreType.DMA
    any_ = pl.BlockSpec(memory_space=pl.ANY)
    vmem = pl.BlockSpec(memory_space=pltpu.VMEM)
    hidden, grad_x, grad_prob = pl.pallas_call(
        functools.partial(mesh_kernel, n, sections),
        out_shape=(
            pltpu.VMEM((slots, units), bf16),
            pltpu.VMEM((tok, width), bf16),
            pltpu.VMEM((top_k, tok), bf16),
        ),
        in_specs=[any_] * 10,
        out_specs=(vmem,) * 3,
        scratch_shapes=[
            pltpu.VMEM((top_k, tok), jnp.int32),
            pltpu.VMEM((top_k, tok), jnp.int32),
            pltpu.VMEM((top_k, tok), jnp.int32),
            pltpu.VMEM((n, tok), bf16),
            pltpu.VMEM((width, units), bf16),
            pltpu.VMEM((width, units), bf16),
            pltpu.VMEM((slots, units), bf16),
            pltpu.VMEM((slots, units), bf16),
            pltpu.VMEM((slots, units), bf16),
            pltpu.VMEM((slots, units), bf16),
            pltpu.VMEM((slots, units), bf16),
            pltpu.VMEM((n, tok, width), bf16),
            pltpu.VMEM((n, tok, width), bf16),
            pltpu.VMEM((n, tok, width), bf16),
            pltpu.VMEM((n, tok, width), bf16),
            pltpu.VMEM((nz, tok, width), bf16),
            pltpu.VMEM((3, tok, width), bf16),
            pltpu.VMEM((n, *small), bf16),
            pltpu.VMEM((n, *small), bf16),
            pltpu.VMEM((n, *small), bf16),
            pltpu.VMEM((n, *small), bf16),
            pltpu.VMEM(small, bf16),
            dma((7,)),
            dma((2, count)),
            dma((count, 4)),
            dma((2, nz, 3)),
            dma((2, nz)),
            dma((3, nz)),
            dma((3, nz)),
            dma((count, 2, nz, 3)),
            dma((count, 2, nz)),
            dma((count, nz)),
            dma((count, nz)),
            dma((count, nz)),
            dma((count, nz)),
            dma((count, nz)),
            dma((count, nz)),
            dma((count, 3)),
            dma((count, 3)),
        ],
        compiler_params=pltpu.CompilerParams(
            collective_id=0, has_side_effects=True, vmem_limit_bytes=VMEM_BYTES
        ),
        name="mesh",
    )(
        x_prev_a[0],
        route_a[0].T,
        prob_a[0].T,
        route_b[0].T,
        prob_b[0, 0],
        w_gate[0],
        w_up[0],
        saved_gate_b.reshape(slots, units),
        saved_up_b.reshape(slots, units),
        grad_hidden_b.reshape(slots, units),
    )
    results = (hidden, grad_x, grad_prob)
    hidden, grad_x, grad_prob = pl.pallas_call(
        put_kernel,
        out_shape=tuple(jax.ShapeDtypeStruct(a.shape, a.dtype) for a in results),
        in_specs=[any_] * 3,
        out_specs=(any_,) * 3,
        scratch_shapes=[dma((3,))],
        compiler_params=pltpu.CompilerParams(vmem_limit_bytes=1 << 20),
        name="put",
    )(*results)
    return (
        hidden.reshape(1, 1, n, tok, units),
        grad_x[None],
        grad_prob.T[None],
    )


def any_routing(*args):
    tokens, top_k = args[1].shape[1:]
    capacity = args[7].shape[3]
    full = top_k == lax.axis_size("expert") and capacity == tokens
    if full and top_k == 8 == ROWS_Y * len(ORDERS) and lax.axis_size("pipe") > 2:
        return full_routing(*args)
    return per_device(*args)


def solution(mesh):
    return jax.shard_map(
        any_routing,
        mesh=mesh,
        in_specs=(
            P("pipe", "expert", None),
            P("pipe", "expert", None),
            P("pipe", "expert", None),
            P("expert", None, None),
            P("expert", None, None),
            P("pipe", "expert", None),
            P("pipe", "expert", None, None),
            P("pipe", "expert", None, None, None),
            P("pipe", "expert", None, None, None),
            P("pipe", "expert", None, None, None),
        ),
        out_specs=(
            P("pipe", "expert", None, None, None),
            P("pipe", "expert", None),
            P("pipe", "expert", None),
        ),
        check_vma=False,
    )
```
